256 devices in a mesh: row: 16 (over x, y), col: 16 (over z, core).
Axes of the slice: x: 4, y: 4, z: 8, core: 2. Of those that a mesh axis runs over, the one named last changes fastest.
Arguments:
- tokens: bfloat16 [192, 192, 768], P('row', 'col'), may hold values from -6 to 6
- w_in: bfloat16 [768, 1536], replicated, may hold values from -0.21875 to 0.21875
- w_xproj: bfloat16 [768, 80], replicated, may hold values from -0.21875 to 0.21875
- w_dt: bfloat16 [48, 768], replicated, may hold values from -0.875 to 0.875
- dt_bias: float32 [768], replicated, may hold values from -7 to -2.3
- a_log: float32 [16, 768], replicated, may hold values from 0 to 2.77
- d_skip: float32 [768], replicated, may hold values from 0.5 to 1.5
- w_out: bfloat16 [768, 768], replicated, may hold values from -0.21875 to 0.21875
- out_grad: bfloat16 [192, 192, 768], P('row', 'col'), may hold values from -6 to 6
Outputs:
- layer_out: bfloat16 [192, 192, 768], P('row', 'col')
- token_grad: bfloat16 [192, 192, 768], P('row', 'col')
The draws below stay inside these ranges and needn't reach their ends.
All inputs are finite; a program needn't handle non-finite values.
Results may differ from the reference program's by a relative error of at most 0.0064.
Values sent between devices are 32-bit elements; how exact they have to be, the bound alone decides.
No kernel may reach another device: no remote copies, remote signals or barrier semaphores. Data moves between devices by JAX's collectives and lax.ppermute only.
A program may use at most 192 MiB of HBM per device.

```python
import jax
import jax.numpy as jnp
from jax import lax

D = 768
STATE = 16
RANK = 48
INNER = 768
ROWS = 192
COLS = 192


def block_scale(stream_key, shape, shards, low, top_value):
    loudness = 1.0
    for position, parts in shards:
        steps = jax.random.uniform(jax.random.fold_in(jax.random.fold_in(stream_key, 6), position), (parts,), jnp.float32, low / len(shards), top_value / len(shards))
        loudness = loudness * jnp.repeat(jnp.exp(steps), shape[position] // parts).reshape((-1,) + (1,) * (len(shape) - 1 - position))
    return loudness


def bell_draw(own_key, extent, deviation, bound, cuts=(), dtype=jnp.bfloat16):
    values = jax.random.normal(own_key, extent, jnp.float32) * deviation
    if len(cuts) > 0:
        values = block_scale(own_key, extent, cuts, -0.22, 0.18) * values
    return jnp.clip(values, min=-bound, max=bound).astype(dtype)


def setup_inputs(seed: int = 0) -> dict:
    key_list = jax.random.split(jax.random.key(seed), 10)
    return {
        "tokens": bell_draw(key_list[0], (ROWS, COLS, D), 1.0, 6.0, ((0, 16), (1, 16))),
        "w_in": bell_draw(key_list[1], (D, 2 * INNER), D ** -0.5, 0.21875),
        "w_xproj": bell_draw(key_list[2], (INNER, RANK + 2 * STATE), INNER ** -0.5, 0.21875),
        "w_dt": bell_draw(key_list[3], (RANK, INNER), RANK ** -0.5, 0.875),
        "dt_bias": jnp.clip(jax.random.uniform(key_list[4], (INNER,), jnp.float32, -7.0, -2.3), -7.0, -2.3),
        "a_log": jnp.clip(jax.random.uniform(key_list[5], (STATE, INNER), jnp.float32, 0.0, 2.77), 0.0, 2.77),
        "d_skip": jnp.clip(jax.random.uniform(key_list[6], (INNER,), jnp.float32, 0.5, 1.5), 0.5, 1.5),
        "w_out": bell_draw(key_list[7], (INNER, D), INNER ** -0.5, 0.21875),
        "out_grad": bell_draw(key_list[8], (ROWS, COLS, D), 1.0, 6.0, ((0, 16), (1, 16))),
    }


channel_block = 16

def compose(earlier, later):
    return (earlier[0] * later[0], later[0] * earlier[1] + later[1])

def silu_grad(values):
    sigmoid = jax.nn.sigmoid(values)
    return sigmoid * (1.0 + values * (1.0 - sigmoid))

def reference(tokens, w_in, w_xproj, w_dt, dt_bias, a_log, d_skip, w_out, out_grad):
    grid_rows, grid_cols, model_width = tokens.shape
    cell_count = grid_rows * grid_cols
    low_rank, inner_width = w_dt.shape
    states = a_log.shape[0]
    flat_tokens = tokens.reshape(cell_count, model_width)
    projected = jnp.dot(flat_tokens, w_in, preferred_element_type=jnp.float32)
    x_pre = projected[:, :inner_width]
    z_pre = projected[:, inner_width:]
    x_act = jax.nn.silu(x_pre).astype(jnp.bfloat16)
    x_dbl = jnp.dot(x_act, w_xproj, preferred_element_type=jnp.float32)
    dt_low = x_dbl[:, :low_rank].astype(jnp.bfloat16)
    b_sel = x_dbl[:, low_rank:low_rank + states]
    c_sel = x_dbl[:, low_rank + states:]
    dt_pre = jnp.dot(dt_low, w_dt, preferred_element_type=jnp.float32) + dt_bias
    step_size = jax.nn.softplus(dt_pre)
    gated_grad = jnp.dot(out_grad.reshape(cell_count, model_width), w_out.T, preferred_element_type=jnp.float32)
    z_silu = jax.nn.silu(z_pre)
    scan_grad = gated_grad * z_silu
    rates = -jnp.exp(a_log)
    step_grid = step_size.reshape(grid_rows, grid_cols, inner_width)
    x_grid = x_act.astype(jnp.float32).reshape(grid_rows, grid_cols, inner_width)
    grad_grid = scan_grad.reshape(grid_rows, grid_cols, inner_width)
    b_grid = b_sel.reshape(grid_rows, grid_cols, states)
    c_grid = c_sel.reshape(grid_rows, grid_cols, states)

    def one_block(block_index, carry):
        scan_out, step_grad, xscan_grad, bsel_grad, csel_grad = carry
        first_channel = (block_index * channel_block).astype(jnp.int32)
        step_part = lax.dynamic_slice_in_dim(step_grid, first_channel, channel_block, 2)
        x_part = lax.dynamic_slice_in_dim(x_grid, first_channel, channel_block, 2)
        grad_part = lax.dynamic_slice_in_dim(grad_grid, first_channel, channel_block, 2)
        rate_part = lax.dynamic_slice_in_dim(rates, first_channel, channel_block, 1)
        skip_part = lax.dynamic_slice_in_dim(d_skip, first_channel, channel_block, 0)
        decays = jnp.exp(step_part[:, :, None, :] * rate_part)
        source = step_part[:, :, None, :] * b_grid[:, :, :, None] * x_part[:, :, None, :]
        row_state = lax.associative_scan(compose, (decays, source), axis=1)[1]
        full_state = lax.associative_scan(compose, (decays, row_state), axis=0)[1]
        out_part = lax.optimization_barrier(jnp.sum(c_grid[:, :, :, None] * full_state, axis=2)) + skip_part * x_part
        state_grad = c_grid[:, :, :, None] * grad_part[:, :, None, :]
        csel_grad = csel_grad + lax.optimization_barrier(jnp.sum(grad_part[:, :, None, :] * full_state, axis=3))
        col_shift = jnp.concatenate([decays[1:], jnp.ones_like(decays[:1])], axis=0)
        col_adjoint = lax.associative_scan(compose, (col_shift, state_grad), axis=0, reverse=True)[1]
        row_shift = jnp.concatenate([decays[:, 1:], jnp.ones_like(decays[:, :1])], axis=1)
        row_adjoint = lax.associative_scan(compose, (row_shift, col_adjoint), axis=1, reverse=True)[1]
        col_before = jnp.concatenate([jnp.zeros_like(full_state[:1]), full_state[:-1]], axis=0)
        row_before = jnp.concatenate([jnp.zeros_like(row_state[:, :1]), row_state[:, :-1]], axis=1)
        decay_grad = col_adjoint * col_before + row_adjoint * row_before
        step_part_grad = lax.optimization_barrier(jnp.sum(decay_grad * decays * rate_part + row_adjoint * b_grid[:, :, :, None] * x_part[:, :, None, :], axis=2))
        bsel_grad = bsel_grad + lax.optimization_barrier(jnp.sum(row_adjoint * step_part[:, :, None, :] * x_part[:, :, None, :], axis=3))
        xscan_part = lax.optimization_barrier(jnp.sum(row_adjoint * step_part[:, :, None, :] * b_grid[:, :, :, None], axis=2)) + grad_part * skip_part
        scan_out = lax.dynamic_update_slice_in_dim(scan_out, out_part, first_channel, 2)
        step_grad = lax.dynamic_update_slice_in_dim(step_grad, step_part_grad, first_channel, 2)
        xscan_grad = lax.dynamic_update_slice_in_dim(xscan_grad, xscan_part, first_channel, 2)
        return (scan_out, step_grad, xscan_grad, bsel_grad, csel_grad)
    wide_zero = jnp.zeros((grid_rows, grid_cols, inner_width), jnp.float32)
    narrow_zero = jnp.zeros((grid_rows, grid_cols, states), jnp.float32)
    scan_out, step_grad, xscan_grad, bsel_grad, csel_grad = lax.fori_loop(0, inner_width // channel_block, one_block, (wide_zero, wide_zero, wide_zero, narrow_zero, narrow_zero))
    scan_flat = scan_out.reshape(cell_count, inner_width)
    gated_out = (scan_flat * z_silu).astype(jnp.bfloat16)
    layer_out = jnp.dot(gated_out, w_out, preferred_element_type=jnp.float32).astype(jnp.bfloat16)
    z_grad = gated_grad * scan_flat * silu_grad(z_pre)
    pre_grad = (step_grad.reshape(cell_count, inner_width) * jax.nn.sigmoid(dt_pre)).astype(jnp.bfloat16)
    low_grad = jnp.dot(pre_grad, w_dt.T, preferred_element_type=jnp.float32)
    dbl_grad = jnp.concatenate([low_grad, bsel_grad.reshape(cell_count, states), csel_grad.reshape(cell_count, states)], axis=1).astype(jnp.bfloat16)
    x_grad = xscan_grad.reshape(cell_count, inner_width) + jnp.dot(dbl_grad, w_xproj.T, preferred_element_type=jnp.float32)
    proj_grad = jnp.concatenate([x_grad * silu_grad(x_pre), z_grad], axis=1).astype(jnp.bfloat16)
    token_grad = jnp.dot(proj_grad, w_in.T, preferred_element_type=jnp.float32).astype(jnp.bfloat16)
    return (layer_out.reshape(grid_rows, grid_cols, model_width), token_grad.reshape(grid_rows, grid_cols, model_width))
```

```python
import jax
import jax.numpy as jnp
from jax import lax
from jax.experimental import pallas as pl
from jax.experimental.pallas import tpu as pltpu
from jax.sharding import PartitionSpec as P

LOG2E = 1.4426950408889634
T = 12
PAD = 16
CELLS = T * PAD
N = 16
C = 768
HALF = 384
LANES = [slice(128 * k, 128 * k + 128) for k in range(C // 128)]
F32, BF16 = jnp.float32, jnp.bfloat16
VMEM_LIMIT = 60 * 1024 * 1024


def nt(left, right):
    return lax.dot_general(left, right, (((1,), (1,)), ((), ())), preferred_element_type=F32)


def blocks():
    for i in range(T):
        for h in range(2):
            q = 2 * i + h
            for half in range(2):
                yield i, h, half, 2 * (q // 3) + half, 8 * (q % 3)


def pack(out_ref, base, edge_ref):
    for i, h, half, chunk, row in blocks():
        out_ref[chunk, base + row : base + row + 8, :] = edge_ref[
            i, 8 * h : 8 * h + 8, HALF * half : HALF * half + HALF
        ]


def unpack(edge_ref, in_ref, base):
    for i, h, half, chunk, row in blocks():
        edge_ref[i, 8 * h : 8 * h + 8, HALF * half : HALF * half + HALF] = in_ref[
            chunk, base + row : base + row + 8, :
        ]


def pack_sums(out_ref, base, sum_rows):
    for chunk in range(16):
        group, half = chunk // 2, chunk % 2
        rows = [
            sum_rows[(3 * group + t) // 2][:, HALF * half : HALF * half + HALF] for t in range(3)
        ]
        out_ref[chunk, base : base + 8, :] = jnp.concatenate(
            rows + [jnp.zeros((5, HALF), F32)], axis=0
        )


def first_kernel(
    tokens_ref, w_in_ref, w_xproj_ref, w_dt_ref, dt_bias_ref, a_log_ref, w_out_ref, out_grad_ref,
    x_pre_ref, z_pre_ref, dt_pre_ref, gated_ref, step_ref, u_ref, x_ref, grad_ref, b_ref, c_ref,
    term_ref, sent_ref,
    tok_s, og_s, rates_s, end_s,
):
    tok_s[...] = jnp.zeros_like(tok_s)
    og_s[...] = jnp.zeros_like(og_s)
    for i in range(T):
        tok_s[i, 0:T, :] = tokens_ref[i]
        og_s[i, 0:T, :] = out_grad_ref[i]
    tok = tok_s[...].reshape(CELLS, C)
    x_pre = jnp.dot(tok, w_in_ref[:, 0:C], preferred_element_type=F32)
    z_pre = jnp.dot(tok, w_in_ref[:, C : 2 * C], preferred_element_type=F32)
    x_pre_ref[...] = x_pre
    z_pre_ref[...] = z_pre
    x_act = (x_pre * jax.nn.sigmoid(x_pre)).astype(BF16)
    x_dbl = jnp.dot(x_act, w_xproj_ref[...], preferred_element_type=F32)
    dt_low = x_dbl[:, 0:48].astype(BF16)
    x_dbl_t = lax.dot_general(
        w_xproj_ref[...], x_act, (((0,), (1,)), ((), ())), preferred_element_type=F32
    )
    for i in range(T):
        for j in range(T):
            cell = PAD * i + j
            b_ref[cell] = jnp.broadcast_to(x_dbl_t[48:64, cell : cell + 1], (N, 128))
            c_ref[cell] = jnp.broadcast_to(x_dbl_t[64:80, cell : cell + 1], (N, 128))
    dt_pre = jnp.dot(dt_low, w_dt_ref[...], preferred_element_type=F32) + dt_bias_ref[...]
    dt_pre_ref[...] = dt_pre
    step = jnp.maximum(dt_pre, 0.0) + jnp.log1p(jnp.exp(-jnp.abs(dt_pre)))
    step_ref[...] = step.reshape(T, PAD, C)
    x_full = x_act.astype(F32)
    x_ref[...] = x_full
    u_ref[...] = (step * x_full).reshape(T, PAD, C)
    gated = nt(og_s[...].reshape(CELLS, C), w_out_ref[...])
    gated_ref[...] = gated
    grad_ref[...] = (gated * (z_pre * jax.nn.sigmoid(z_pre))).reshape(T, PAD, C)
    rates_s[...] = -jnp.exp(a_log_ref[...]) * LOG2E
    term_ref[...] = jnp.zeros_like(term_ref)

    def one_row(back, carry):
        i = T - 1 - back
        row = [jnp.zeros((N, 128), F32) for _ in LANES]
        for j in range(T):
            b = b_ref[PAD * i + j]
            c = c_ref[PAD * i + j]
            for k, lanes in enumerate(LANES):
                decay = jnp.exp2(rates_s[:, lanes] * step_ref[i, j : j + 1, lanes])
                row[k] = decay * row[k] + b * u_ref[i, j : j + 1, lanes]
                term_ref[j, :, lanes] = decay * (
                    c * grad_ref[i, j : j + 1, lanes] + term_ref[j, :, lanes]
                )
        for k, lanes in enumerate(LANES):
            end_s[i, :, lanes] = row[k]
        return carry

    lax.fori_loop(0, T, one_row, 0)
    pack(sent_ref, 0, end_s)
    pack_sums(
        sent_ref, 24, [jnp.sum(step_ref[i, 0:T, :], axis=0, keepdims=True) for i in range(T)]
    )


def prefix_kernel(axis, spans, sum_base, got_ref, sums_ref, a_log_ref, out_ref):
    me = lax.axis_index(axis)
    group, half = me // 2, me % 2
    for t in range(3):
        state_rows = pl.multiple_of(8 * ((3 * group + t) % 2), 8)
        lanes = pl.multiple_of(HALF * half, 128)
        rate = -jnp.exp(a_log_ref[pl.ds(state_rows, 8), pl.ds(lanes, HALF)]) * LOG2E
        for base, reverse in spans:
            state = jnp.zeros((8, HALF), F32)
            rows = slice(base + 8 * t, base + 8 * t + 8)
            for hop in range(16):
                tile = 15 - hop if reverse else hop
                out_ref[tile, rows, :] = state
                decay = jnp.exp2(rate * sums_ref[tile, sum_base + t : sum_base + t + 1, :])
                state = decay * state + got_ref[tile, rows, :]


def forward_kernel(
    row_in_ref, a_log_ref, step_ref, u_ref, b_ref, term_ref, sent_ref, rates_s, row_s, col_s
):
    rates_s[...] = -jnp.exp(a_log_ref[...]) * LOG2E
    unpack(row_s, row_in_ref, 0)
    col_s[...] = jnp.zeros_like(col_s)

    def one_row(i, carry):
        row = [row_s[i, :, lanes] for lanes in LANES]
        for j in range(T):
            b = b_ref[PAD * i + j]
            for k, lanes in enumerate(LANES):
                decay = jnp.exp2(rates_s[:, lanes] * step_ref[i, j : j + 1, lanes])
                row[k] = decay * row[k] + b * u_ref[i, j : j + 1, lanes]
                col_s[j, :, lanes] = decay * col_s[j, :, lanes] + row[k]
        return carry

    lax.fori_loop(0, T, one_row, 0)
    pack(sent_ref, 0, col_s)
    pack(sent_ref, 24, term_ref)
    total = step_ref[0]
    for i in range(1, T):
        total = total + step_ref[i]
    pack_sums(sent_ref, 48, [total[j : j + 1, :] for j in range(T)])


def backward_kernel(
    col_got_ref, a_log_ref, step_ref, grad_ref, c_ref, sent_ref, rates_s, term_s, end_s
):
    rates_s[...] = -jnp.exp(a_log_ref[...]) * LOG2E
    unpack(term_s, col_got_ref, 24)

    def one_row(back, carry):
        i = T - 1 - back
        row = [jnp.zeros((N, 128), F32) for _ in LANES]
        for j in reversed(range(T)):
            c = c_ref[PAD * i + j]
            for k, lanes in enumerate(LANES):
                decay = jnp.exp2(rates_s[:, lanes] * step_ref[i, j : j + 1, lanes])
                adjoint = c * grad_ref[i, j : j + 1, lanes] + term_s[j, :, lanes]
                term_s[j, :, lanes] = decay * adjoint
                row[k] = decay * (adjoint + row[k])
        for k, lanes in enumerate(LANES):
            end_s[i, :, lanes] = row[k]
        return carry

    lax.fori_loop(0, T, one_row, 0)
    pack(sent_ref, 0, end_s)


def last_kernel(
    row_in_ref, col_got_ref, row_from_ref, x_pre_ref, z_pre_ref, dt_pre_ref, gated_ref, step_ref,
    u_ref, x_ref, grad_ref, b_ref, c_ref, a_log_ref, d_skip_ref, w_in_ref, w_xproj_ref, w_dt_ref,
    w_out_ref,
    layer_ref, token_ref,
    rates_s, row_s, col_s, full_keep, row_keep, scan_s, step_sum_s, x_sum_s, b_part, c_part, w_dt_s,
):
    neg_rates = -jnp.exp(a_log_ref[...])
    rates_s[...] = neg_rates * LOG2E
    unpack(row_s, row_in_ref, 0)
    unpack(col_s, col_got_ref, 0)
    for ref in (scan_s, step_sum_s, x_sum_s, b_part, c_part):
        ref[...] = jnp.zeros_like(ref)

    def down_row(i, carry):
        row = [row_s[i, :, lanes] for lanes in LANES]
        for j in range(T):
            cell = PAD * i + j
            b = b_ref[cell]
            c = c_ref[cell]
            part = jnp.zeros((N, 128), F32)
            for k, lanes in enumerate(LANES):
                decay = jnp.exp2(rates_s[:, lanes] * step_ref[i, j : j + 1, lanes])
                row_old = decay * row[k]
                row[k] = row_old + b * u_ref[i, j : j + 1, lanes]
                full_old = decay * col_s[j, :, lanes]
                full = full_old + row[k]
                col_s[j, :, lanes] = full
                row_keep[cell, :, lanes] = row_old
                full_keep[cell, :, lanes] = full_old
                scan_s[i, j : j + 1, lanes] = jnp.sum(c * full, axis=0, keepdims=True)
                part = part + full * grad_ref[i, j : j + 1, lanes]
            c_part[cell] = part
        return carry

    lax.fori_loop(0, T, down_row, 0)
    unpack(col_s, col_got_ref, 24)
    unpack(row_s, row_from_ref, 0)

    def up_row(back, carry):
        i = T - 1 - back
        row = [row_s[i, :, lanes] for lanes in LANES]
        for j in reversed(range(T)):
            cell = PAD * i + j
            b = b_ref[cell]
            c = c_ref[cell]
            part = jnp.zeros((N, 128), F32)
            for k, lanes in enumerate(LANES):
                decay = jnp.exp2(rates_s[:, lanes] * step_ref[i, j : j + 1, lanes])
                col_adjoint = c * grad_ref[i, j : j + 1, lanes] + col_s[j, :, lanes]
                col_s[j, :, lanes] = decay * col_adjoint
                row_adjoint = col_adjoint + row[k]
                row[k] = decay * row_adjoint
                decay_grad = (
                    col_adjoint * full_keep[cell, :, lanes] + row_adjoint * row_keep[cell, :, lanes]
                )
                step_sum_s[i, j : j + 1, lanes] = jnp.sum(
                    decay_grad * rates_s[:, lanes], axis=0, keepdims=True
                )
                x_sum_s[i, j : j + 1, lanes] = jnp.sum(row_adjoint * b, axis=0, keepdims=True)
                part = part + row_adjoint * u_ref[i, j : j + 1, lanes]
            b_part[cell] = part
        return carry

    lax.fori_loop(0, T, up_row, 0)

    x = x_ref[...]
    z_pre = z_pre_ref[...]
    x_pre = x_pre_ref[...]
    skip = d_skip_ref[...]
    step = step_ref[...].reshape(CELLS, C)
    grad = grad_ref[...].reshape(CELLS, C)
    scan_out = scan_s[...].reshape(CELLS, C) + skip * x
    z_sig = jax.nn.sigmoid(z_pre)
    gated_out = (scan_out * (z_pre * z_sig)).astype(BF16)
    layer = jnp.dot(gated_out, w_out_ref[...], preferred_element_type=F32).astype(BF16)
    for i in range(T):
        layer_ref[i] = layer[PAD * i : PAD * i + T, :]
    z_grad = (gated_ref[...] * scan_out * (z_sig * (1.0 + z_pre * (1.0 - z_sig)))).astype(BF16)
    x_sum = x_sum_s[...].reshape(CELLS, C)
    step_grad = step_sum_s[...].reshape(CELLS, C) * (1.0 / LOG2E) + x_sum * x
    pre_grad = (step_grad * jax.nn.sigmoid(dt_pre_ref[...])).astype(BF16)
    w_dt_s[...] = jnp.zeros_like(w_dt_s)
    w_dt_s[0:48, :] = w_dt_ref[...]
    low = nt(pre_grad, w_dt_s[...])
    rows = lax.broadcasted_iota(jnp.int32, (CELLS * N, 80), 0)
    cols = lax.broadcasted_iota(jnp.int32, (CELLS * N, 80), 1)
    state = rows % N
    b_sum = jnp.sum(b_part[...].reshape(CELLS * N, 128), axis=1, keepdims=True)
    c_sum = jnp.sum(c_part[...].reshape(CELLS * N, 128), axis=1, keepdims=True)
    placed = jnp.where(cols == state + 48, b_sum, jnp.where(cols == state + 64, c_sum, 0.0))
    owner = lax.broadcasted_iota(jnp.int32, (CELLS, CELLS * N), 1) // N
    cell = lax.broadcasted_iota(jnp.int32, (CELLS, CELLS * N), 0)
    choose = (owner == cell).astype(F32).astype(BF16)
    dbl = (low + jnp.dot(choose, placed.astype(BF16), preferred_element_type=F32)).astype(BF16)
    x_grad = x_sum * step + grad * skip + nt(dbl, w_xproj_ref[...])
    x_sig = jax.nn.sigmoid(x_pre)
    x_part = (x_grad * (x_sig * (1.0 + x_pre * (1.0 - x_sig)))).astype(BF16)
    token = (nt(x_part, w_in_ref[:, 0:C]) + nt(z_grad, w_in_ref[:, C : 2 * C])).astype(BF16)
    for i in range(T):
        token_ref[i] = token[PAD * i : PAD * i + T, :]


def call(kernel, out_shape, scratch, name):
    return pl.pallas_call(
        kernel,
        out_shape=out_shape,
        scratch_shapes=scratch,
        name=name,
        compiler_params=pltpu.CompilerParams(vmem_limit_bytes=VMEM_LIMIT),
    )


def f32(*shape):
    return jax.ShapeDtypeStruct(shape, F32)


def vmem(*shape):
    return pltpu.VMEM(shape, F32)


def prefix(axis, spans, sum_base, rows, got, sums, a_log):
    def kernel(got_ref, sums_ref, a_log_ref, out_ref):
        prefix_kernel(axis, spans, sum_base, got_ref, sums_ref, a_log_ref, out_ref)

    return call(kernel, f32(16, rows, HALF), (), "prefix_" + axis)(got, sums, a_log)


def swap(sent, axis):
    return lax.all_to_all(sent, axis, 0, 0, tiled=True)


def body(tokens, w_in, w_xproj, w_dt, dt_bias, a_log, d_skip, w_out, out_grad):
    edge = vmem(T, N, C)
    (x_pre, z_pre, dt_pre, gated, step, u, x, grad, b, c, term, row_sent) = call(
        first_kernel,
        (
            f32(CELLS, C), f32(CELLS, C), f32(CELLS, C), f32(CELLS, C),
            f32(T, PAD, C), f32(T, PAD, C), f32(CELLS, C), f32(T, PAD, C),
            f32(CELLS, N, 128), f32(CELLS, N, 128), f32(T, N, C), f32(16, 32, HALF),
        ),
        (pltpu.VMEM((T, PAD, C), BF16), pltpu.VMEM((T, PAD, C), BF16), vmem(N, C), edge),
        "first",
    )(tokens, w_in, w_xproj, w_dt, dt_bias.reshape(1, C), a_log, w_out, out_grad)
    row_got = swap(row_sent, "col")
    row_in = swap(prefix("col", ((0, False),), 24, 24, row_got, row_got, a_log), "col")
    col_sent = call(
        forward_kernel, f32(16, 56, HALF), (vmem(N, C), edge, edge), "forward"
    )(row_in, a_log, step, u, b, term)
    col_all = swap(col_sent, "row")
    col_got = swap(
        prefix("row", ((0, False), (24, True)), 48, 48, col_all, col_all, a_log), "row"
    )
    back_sent = call(
        backward_kernel, f32(16, 24, HALF), (vmem(N, C), edge, edge), "backward"
    )(col_got, a_log, step, grad, c)
    back_all = swap(back_sent, "col")
    row_from = swap(prefix("col", ((0, True),), 24, 24, back_all, row_got, a_log), "col")
    out = jax.ShapeDtypeStruct((T, T, C), BF16)
    wide = vmem(T, PAD, C)
    return call(
        last_kernel,
        (out, out),
        (
            vmem(N, C), edge, edge, vmem(CELLS, N, C), vmem(CELLS, N, C), wide, wide, wide,
            vmem(CELLS, N, 128), vmem(CELLS, N, 128), pltpu.VMEM((80, C), BF16),
        ),
        "last",
    )(
        row_in, col_got, row_from, x_pre, z_pre, dt_pre, gated, step, u, x, grad, b, c, a_log,
        d_skip.reshape(1, C), w_in, w_xproj, w_dt, w_out,
    )


def solution(mesh):
    return jax.shard_map(
        body,
        mesh=mesh,
        in_specs=(P("row", "col", None), P(), P(), P(), P(), P(), P(), P(), P("row", "col", None)),
        out_specs=(P("row", "col", None), P("row", "col", None)),
        check_vma=False,
    )
```

```python
import jax
import jax.numpy as jnp
from jax import lax
from jax.experimental import pallas as pl
from jax.experimental.pallas import tpu as pltpu
from jax.sharding import PartitionSpec as P

LOG2E = 1.4426950408889634
T = 12
PAD = 16
CELLS = T * PAD
N = 16
C = 768
HALF = 384
LANES = [slice(128 * k, 128 * k + 128) for k in range(C // 128)]
F32, BF16 = jnp.float32, jnp.bfloat16


def nt(left, right):
    return lax.dot_general(left, right, (((1,), (1,)), ((), ())), preferred_element_type=F32)


def blocks():
    for i in range(T):
        for h in range(2):
            q = 2 * i + h
            for half in range(2):
                yield i, h, half, 2 * (q // 3) + half, 8 * (q % 3)


def pack(out_ref, base, edge_ref):
    for i, h, half, chunk, row in blocks():
        out_ref[chunk, base + row : base + row + 8, :] = edge_ref[
            i, 8 * h : 8 * h + 8, HALF * half : HALF * half + HALF
        ]


def unpack(edge_ref, in_ref, base):
    for i, h, half, chunk, row in blocks():
        edge_ref[i, 8 * h : 8 * h + 8, HALF * half : HALF * half + HALF] = in_ref[
            chunk, base + row : base + row + 8, :
        ]


def pack_sums(out_ref, base, sum_rows):
    for chunk in range(16):
        group, half = chunk // 2, chunk % 2
        rows = [
            sum_rows[(3 * group + t) // 2][:, HALF * half : HALF * half + HALF] for t in range(3)
        ]
        out_ref[chunk, base : base + 8, :] = jnp.concatenate(
            rows + [jnp.zeros((5, HALF), F32)], axis=0
        )


def fetch(pairs, sems):
    copies = [pltpu.make_async_copy(src, dst, sems.at[k]) for k, (src, dst) in enumerate(pairs)]
    for copy in copies:
        copy.start()
    return copies


def first_kernel(
    tokens_hbm, w_in_hbm, w_xproj_hbm, w_dt_hbm, a_log_hbm, w_out_hbm, out_grad_hbm, dt_bias_ref,
    x_pre_ref, z_pre_ref, dt_pre_ref, gated_ref, step_ref, u_ref, x_ref, grad_ref, b_ref, c_ref,
    term_ref, rates_ref, sent_ref,
    tokens_ref, w_x_ref, w_z_ref, w_xproj_ref, w_dt_ref, a_log_ref, w_out_ref, out_grad_ref,
    tok_s, og_s, end_s, sems,
):
    copies = fetch(
        (
            (tokens_hbm, tokens_ref),
            (w_in_hbm.at[:, 0:C], w_x_ref),
            (w_xproj_hbm, w_xproj_ref),
            (w_dt_hbm, w_dt_ref),
            (a_log_hbm, a_log_ref),
            (w_in_hbm.at[:, C : 2 * C], w_z_ref),
            (out_grad_hbm, out_grad_ref),
            (w_out_hbm, w_out_ref),
        ),
        sems,
    )
    tok_s[...] = jnp.zeros_like(tok_s)
    og_s[...] = jnp.zeros_like(og_s)
    copies[0].wait()
    for i in range(T):
        tok_s[i, 0:T, :] = tokens_ref[i]
    tok = tok_s[...].reshape(CELLS, C)
    copies[1].wait()
    x_pre = jnp.dot(tok, w_x_ref[...], preferred_element_type=F32)
    x_pre_ref[...] = x_pre
    x_act = (x_pre * jax.nn.sigmoid(x_pre)).astype(BF16)
    copies[2].wait()
    dt_low = nt(x_act, w_xproj_ref[...])[:, 0:48].astype(BF16)
    x_dbl_t = nt(w_xproj_ref[...], x_act)
    for i in range(T):
        for j in range(T):
            cell = PAD * i + j
            b_ref[cell] = jnp.broadcast_to(x_dbl_t[48:64, cell : cell + 1], (N, 128))
            c_ref[cell] = jnp.broadcast_to(x_dbl_t[64:80, cell : cell + 1], (N, 128))
    copies[3].wait()
    dt_pre = jnp.dot(dt_low, w_dt_ref[...], preferred_element_type=F32) + dt_bias_ref[...]
    dt_pre_ref[...] = dt_pre
    step = jnp.maximum(dt_pre, 0.0) + jnp.log1p(jnp.exp(-jnp.abs(dt_pre)))
    step_ref[...] = step.reshape(T, PAD, C)
    x_full = x_act.astype(F32)
    x_ref[...] = x_full
    u_ref[...] = (step * x_full).reshape(T, PAD, C)
    copies[4].wait()
    rates_ref[...] = -jnp.exp(a_log_ref[...]) * LOG2E
    copies[5].wait()
    z_pre = jnp.dot(tok, w_z_ref[...], preferred_element_type=F32)
    z_pre_ref[...] = z_pre
    copies[6].wait()
    for i in range(T):
        og_s[i, 0:T, :] = out_grad_ref[i]
    copies[7].wait()
    gated = nt(og_s[...].reshape(CELLS, C), w_out_ref[...])
    gated_ref[...] = gated
    grad_ref[...] = (gated * (z_pre * jax.nn.sigmoid(z_pre))).reshape(T, PAD, C)
    term_ref[...] = jnp.zeros_like(term_ref)

    def one_row(back, carry):
        i = T - 1 - back
        row = [jnp.zeros((N, 128), F32) for _ in LANES]
        for j in range(T):
            b = b_ref[PAD * i + j]
            c = c_ref[PAD * i + j]
            for k, lanes in enumerate(LANES):
                decay = jnp.exp2(rates_ref[:, lanes] * step_ref[i, j : j + 1, lanes])
                row[k] = decay * row[k] + b * u_ref[i, j : j + 1, lanes]
                term_ref[j, :, lanes] = decay * (
                    c * grad_ref[i, j : j + 1, lanes] + term_ref[j, :, lanes]
                )
        for k, lanes in enumerate(LANES):
            end_s[i, :, lanes] = row[k]
        return carry

    lax.fori_loop(0, T, one_row, 0)
    pack(sent_ref, 0, end_s)
    pack_sums(
        sent_ref, 24, [jnp.sum(step_ref[i, 0:T, :], axis=0, keepdims=True) for i in range(T)]
    )


def prefix_kernel(axis, spans, sum_base, got_ref, sums_ref, rates_ref, out_ref):
    me = lax.axis_index(axis)
    group, half = me // 2, me % 2
    for t in range(3):
        state_rows = pl.multiple_of(8 * ((3 * group + t) % 2), 8)
        lanes = pl.multiple_of(HALF * half, 128)
        rate = rates_ref[pl.ds(state_rows, 8), pl.ds(lanes, HALF)]
        for base, reverse in spans:
            state = jnp.zeros((8, HALF), F32)
            rows = slice(base + 8 * t, base + 8 * t + 8)
            for hop in range(16):
                tile = 15 - hop if reverse else hop
                out_ref[tile, rows, :] = state
                decay = jnp.exp2(rate * sums_ref[tile, sum_base + t : sum_base + t + 1, :])
                state = decay * state + got_ref[tile, rows, :]


def forward_kernel(
    row_in_ref, rates_s, step_ref, u_ref, b_ref, term_ref, sent_ref, row_s, col_s
):
    unpack(row_s, row_in_ref, 0)
    col_s[...] = jnp.zeros_like(col_s)

    def one_row(i, carry):
        row = [row_s[i, :, lanes] for lanes in LANES]
        for j in range(T):
            b = b_ref[PAD * i + j]
            for k, lanes in enumerate(LANES):
                decay = jnp.exp2(rates_s[:, lanes] * step_ref[i, j : j + 1, lanes])
                row[k] = decay * row[k] + b * u_ref[i, j : j + 1, lanes]
                col_s[j, :, lanes] = decay * col_s[j, :, lanes] + row[k]
        return carry

    lax.fori_loop(0, T, one_row, 0)
    pack(sent_ref, 0, col_s)
    pack(sent_ref, 24, term_ref)
    total = step_ref[0]
    for i in range(1, T):
        total = total + step_ref[i]
    pack_sums(sent_ref, 48, [total[j : j + 1, :] for j in range(T)])


def backward_kernel(
    col_got_ref, rates_s, step_ref, grad_ref, c_ref, sent_ref, term_s, end_s
):
    unpack(term_s, col_got_ref, 24)

    def one_row(back, carry):
        i = T - 1 - back
        row = [jnp.zeros((N, 128), F32) for _ in LANES]
        for j in reversed(range(T)):
            c = c_ref[PAD * i + j]
            for k, lanes in enumerate(LANES):
                decay = jnp.exp2(rates_s[:, lanes] * step_ref[i, j : j + 1, lanes])
                adjoint = c * grad_ref[i, j : j + 1, lanes] + term_s[j, :, lanes]
                term_s[j, :, lanes] = decay * adjoint
                row[k] = decay * (adjoint + row[k])
        for k, lanes in enumerate(LANES):
            end_s[i, :, lanes] = row[k]
        return carry

    lax.fori_loop(0, T, one_row, 0)
    pack(sent_ref, 0, end_s)


def last_kernel(
    row_in_ref, col_got_ref, row_from_ref, x_pre_ref, z_pre_ref, dt_pre_ref, gated_ref, step_ref,
    u_ref, x_ref, grad_ref, b_ref, c_ref, rates_s, d_skip_ref, w_in_hbm, w_xproj_hbm, w_dt_hbm,
    w_out_hbm,
    layer_hbm, token_hbm,
    w_in_ref, w_xproj_ref, w_dt_ref, w_out_ref, layer_ref, token_ref,
    row_s, col_s, full_keep, row_keep, scan_s, step_sum_s, x_sum_s, b_part, c_part, w_dt_s, sems,
):
    copies = fetch(
        (
            (w_out_hbm, w_out_ref),
            (w_dt_hbm, w_dt_ref),
            (w_xproj_hbm, w_xproj_ref),
            (w_in_hbm, w_in_ref),
        ),
        sems,
    )
    unpack(row_s, row_in_ref, 0)
    unpack(col_s, col_got_ref, 0)
    for ref in (scan_s, step_sum_s, x_sum_s, b_part, c_part):
        ref[...] = jnp.zeros_like(ref)

    def down_row(i, carry):
        row = [row_s[i, :, lanes] for lanes in LANES]
        for j in range(T):
            cell = PAD * i + j
            b = b_ref[cell]
            c = c_ref[cell]
            part = jnp.zeros((N, 128), F32)
            for k, lanes in enumerate(LANES):
                decay = jnp.exp2(rates_s[:, lanes] * step_ref[i, j : j + 1, lanes])
                row_old = decay * row[k]
                row[k] = row_old + b * u_ref[i, j : j + 1, lanes]
                full_old = decay * col_s[j, :, lanes]
                full = full_old + row[k]
                col_s[j, :, lanes] = full
                row_keep[T * i + j, :, lanes] = row_old
                full_keep[T * i + j, :, lanes] = full_old
                scan_s[i, j : j + 1, lanes] = jnp.sum(c * full, axis=0, keepdims=True)
                part = part + full * grad_ref[i, j : j + 1, lanes]
            c_part[cell] = part
        return carry

    lax.fori_loop(0, T, down_row, 0)
    x = x_ref[...]
    z_pre = z_pre_ref[...]
    skip = d_skip_ref[...]
    scan_out = scan_s[...].reshape(CELLS, C) + skip * x
    z_sig = jax.nn.sigmoid(z_pre)
    gated_out = (scan_out * (z_pre * z_sig)).astype(BF16)
    copies[0].wait()
    layer = jnp.dot(gated_out, w_out_ref[...], preferred_element_type=F32).astype(BF16)
    for i in range(T):
        layer_ref[i] = layer[PAD * i : PAD * i + T, :]
    layer_copy = pltpu.make_async_copy(layer_ref, layer_hbm, sems.at[4])
    layer_copy.start()
    scan_s[...] = (gated_ref[...] * scan_out * (z_sig * (1.0 + z_pre * (1.0 - z_sig)))).reshape(
        T, PAD, C
    )
    unpack(col_s, col_got_ref, 24)
    unpack(row_s, row_from_ref, 0)

    def up_row(back, carry):
        i = T - 1 - back
        row = [row_s[i, :, lanes] for lanes in LANES]
        for j in reversed(range(T)):
            cell = PAD * i + j
            b = b_ref[cell]
            c = c_ref[cell]
            part = jnp.zeros((N, 128), F32)
            for k, lanes in enumerate(LANES):
                decay = jnp.exp2(rates_s[:, lanes] * step_ref[i, j : j + 1, lanes])
                col_adjoint = c * grad_ref[i, j : j + 1, lanes] + col_s[j, :, lanes]
                col_s[j, :, lanes] = decay * col_adjoint
                row_adjoint = col_adjoint + row[k]
                row[k] = decay * row_adjoint
                decay_grad = (
                    col_adjoint * full_keep[T * i + j, :, lanes] + row_adjoint * row_keep[T * i + j, :, lanes]
                )
                step_sum_s[i, j : j + 1, lanes] = jnp.sum(
                    decay_grad * rates_s[:, lanes], axis=0, keepdims=True
                )
                x_sum_s[i, j : j + 1, lanes] = jnp.sum(row_adjoint * b, axis=0, keepdims=True)
                part = part + row_adjoint * u_ref[i, j : j + 1, lanes]
            b_part[cell] = part
        return carry

    lax.fori_loop(0, T, up_row, 0)

    x = x_ref[...]
    x_pre = x_pre_ref[...]
    step = step_ref[...].reshape(CELLS, C)
    grad = grad_ref[...].reshape(CELLS, C)
    x_sum = x_sum_s[...].reshape(CELLS, C)
    step_grad = step_sum_s[...].reshape(CELLS, C) * (1.0 / LOG2E) + x_sum * x
    pre_grad = (step_grad * jax.nn.sigmoid(dt_pre_ref[...])).astype(BF16)
    copies[1].wait()
    w_dt_s[...] = jnp.zeros_like(w_dt_s)
    w_dt_s[0:48, :] = w_dt_ref[...]
    low = nt(pre_grad, w_dt_s[...])
    rows = lax.broadcasted_iota(jnp.int32, (CELLS * N, 80), 0)
    cols = lax.broadcasted_iota(jnp.int32, (CELLS * N, 80), 1)
    state = rows % N
    b_sum = jnp.sum(b_part[...].reshape(CELLS * N, 128), axis=1, keepdims=True)
    c_sum = jnp.sum(c_part[...].reshape(CELLS * N, 128), axis=1, keepdims=True)
    placed = jnp.where(cols == state + 48, b_sum, jnp.where(cols == state + 64, c_sum, 0.0))
    owner = lax.broadcasted_iota(jnp.int32, (CELLS, CELLS * N), 1) // N
    cell = lax.broadcasted_iota(jnp.int32, (CELLS, CELLS * N), 0)
    choose = (owner == cell).astype(F32).astype(BF16)
    dbl = (low + jnp.dot(choose, placed.astype(BF16), preferred_element_type=F32)).astype(BF16)
    copies[2].wait()
    x_grad = (
        x_sum * step
        + grad * d_skip_ref[...]
        + jnp.dot(dbl, w_xproj_ref[...], preferred_element_type=F32)
    )
    x_sig = jax.nn.sigmoid(x_pre)
    x_part = (x_grad * (x_sig * (1.0 + x_pre * (1.0 - x_sig)))).astype(BF16)
    z_part = scan_s[...].reshape(CELLS, C).astype(BF16)
    copies[3].wait()
    token = (nt(x_part, w_in_ref[:, 0:C]) + nt(z_part, w_in_ref[:, C : 2 * C])).astype(BF16)
    for i in range(T):
        token_ref[i] = token[PAD * i : PAD * i + T, :]
    token_copy = pltpu.make_async_copy(token_ref, token_hbm, sems.at[5])
    token_copy.start()
    layer_copy.wait()
    token_copy.wait()


IN_VMEM = pl.BlockSpec(memory_space=pltpu.VMEM)
IN_HBM = pl.BlockSpec(memory_space=pltpu.HBM)


def call(kernel, out_shape, scratch, name, limit, *args, fetched=(), out_spec=IN_VMEM):
    many = isinstance(out_shape, tuple)
    return pl.pallas_call(
        kernel,
        out_shape=out_shape,
        in_specs=[IN_HBM if k in fetched else IN_VMEM for k in range(len(args))],
        out_specs=tuple(out_spec for _ in out_shape) if many else out_spec,
        scratch_shapes=scratch,
        name=name,
        compiler_params=pltpu.CompilerParams(vmem_limit_bytes=limit * 1024 * 1024),
    )(*args)


def f32(*shape):
    return jax.ShapeDtypeStruct(shape, F32)


def vmem(*shape):
    return pltpu.VMEM(shape, F32)


def prefix(axis, spans, sum_base, rows, got, sums, rates):
    def kernel(got_ref, sums_ref, rates_ref, out_ref):
        prefix_kernel(axis, spans, sum_base, got_ref, sums_ref, rates_ref, out_ref)

    return call(kernel, f32(16, rows, HALF), (), "prefix_" + axis, 4, got, sums, rates)


def swap(sent, axis):
    return lax.all_to_all(sent, axis, 0, 0, tiled=True)


def body(tokens, w_in, w_xproj, w_dt, dt_bias, a_log, d_skip, w_out, out_grad):
    edge, wide = vmem(T, N, C), vmem(T, PAD, C)
    flat, grid, spread = f32(CELLS, C), f32(T, PAD, C), f32(CELLS, N, 128)
    kept = vmem(T * T, N, C)
    padded, cells = pltpu.VMEM((T, PAD, C), BF16), pltpu.VMEM((T, T, C), BF16)
    square, narrow = pltpu.VMEM((C, C), BF16), pltpu.VMEM((80, C), BF16)
    low_rank = pltpu.VMEM((48, C), BF16)
    w_xproj = w_xproj.T
    x_pre, z_pre, dt_pre, gated, step, u, x, grad, b, c, term, rates, row_sent = call(
        first_kernel,
        (
            flat, flat, flat, flat, grid, grid, flat, grid, spread, spread, f32(T, N, C),
            f32(N, C), f32(16, 32, HALF),
        ),
        (
            cells, square, square, narrow, low_rank, vmem(N, C), square, cells,
            padded, padded, edge, pltpu.SemaphoreType.DMA((8,)),
        ),
        "first", 54,
        tokens, w_in, w_xproj, w_dt, a_log, w_out, out_grad, dt_bias,
        fetched=range(7),
    )
    row_got = swap(row_sent, "col")
    row_in = swap(prefix("col", ((0, False),), 24, 24, row_got, row_got, rates), "col")
    col_sent = call(
        forward_kernel, f32(16, 56, HALF), (edge, edge), "forward", 6,
        row_in, rates, step, u, b, term,
    )
    col_all = swap(col_sent, "row")
    col_got = swap(
        prefix("row", ((0, False), (24, True)), 48, 48, col_all, col_all, rates), "row"
    )
    back_sent = call(
        backward_kernel, f32(16, 24, HALF), (edge, edge), "backward", 6,
        col_got, rates, step, grad, c,
    )
    back_all = swap(back_sent, "col")
    row_from = swap(prefix("col", ((0, True),), 24, 24, back_all, row_got, rates), "col")
    out = jax.ShapeDtypeStruct((T, T, C), BF16)
    return call(
        last_kernel,
        (out, out),
        (
            pltpu.VMEM((C, 2 * C), BF16), narrow, low_rank, square, cells, cells,
            edge, edge, kept, kept, wide, wide, wide,
            vmem(CELLS, N, 128), vmem(CELLS, N, 128), narrow, pltpu.SemaphoreType.DMA((6,)),
        ),
        "last", 42,
        row_in, col_got, row_from, x_pre, z_pre, dt_pre, gated, step, u, x, grad, b, c, rates,
        d_skip, w_in, w_xproj, w_dt, w_out,
        fetched=range(15, 19), out_spec=IN_HBM,
    )


def solution(mesh):
    return jax.shard_map(
        body,
        mesh=mesh,
        in_specs=(P("row", "col", None), P(), P(), P(), P(), P(), P(), P(), P("row", "col", None)),
        out_specs=(P("row", "col", None), P("row", "col", None)),
        check_vma=False,
    )
```

```python
import jax
import jax.numpy as jnp
from jax import lax
from jax.experimental import pallas as pl
from jax.experimental.pallas import tpu as pltpu
from jax.sharding import PartitionSpec as P

LOG2E = 1.4426950408889634
T = 12
PAD = 16
CELLS = T * PAD
N = 16
C = 768
HALF = 384
LANES = [slice(128 * k, 128 * k + 128) for k in range(C // 128)]
F32, BF16 = jnp.float32, jnp.bfloat16


def nt(left, right):
    return lax.dot_general(left, right, (((1,), (1,)), ((), ())), preferred_element_type=F32)


def pieces():
    for i in range(T):
        for h in range(2):
            q = 2 * i + h
            for k in range(3):
                yield i, slice(8 * h, 8 * h + 8), k, q // 3, 8 * (3 * (q % 3) + k)


def half_lanes(half, k):
    if isinstance(half, int):
        return slice(HALF * half + 128 * k, HALF * half + 128 * k + 128)
    return pl.ds(pl.multiple_of(HALF * half + 128 * k, 128), 128)


def pack_half(chunk_of, base, edge_ref, half):
    for i, states, k, group, row in pieces():
        chunk_of(group)[base + row : base + row + 8, :] = edge_ref[i, states, half_lanes(half, k)]


def unpack_half(edge_ref, chunk_of, base, half):
    for i, states, k, group, row in pieces():
        edge_ref[i, states, half_lanes(half, k)] = chunk_of(group)[base + row : base + row + 8, :]


def pack_sums(chunk_of, base, sum_ref, half):
    for group in range(8):
        rows = [
            sum_ref[pl.ds(3 * group // 2 + u, 1), half_lanes(half, k)]
            for u in range(2)
            for k in range(3)
        ]
        chunk_of(group)[base : base + 8, :] = jnp.concatenate(
            rows + [jnp.zeros((2, 128), F32)], axis=0
        )


def both_halves(ref):
    return [(lambda group, half=half: ref.at[2 * group + half]) for half in range(2)]


def one_half(ref):
    return lambda group: ref.at[group]


def fetch(pairs, sems):
    copies = [pltpu.make_async_copy(src, dst, sems.at[k]) for k, (src, dst) in enumerate(pairs)]
    for copy in copies:
        copy.start()
    return copies


def first_kernel(
    tokens_hbm, w_in_hbm, w_xproj_hbm, w_dt_hbm, a_log_hbm, w_out_hbm, out_grad_hbm, dt_bias_ref,
    x_pre_ref, z_pre_ref, dt_pre_ref, gated_ref, step_ref, u_ref, x_ref, grad_ref, b_ref, c_ref,
    term_ref, rates_ref, own_ref, other_ref,
    tokens_ref, w_x_ref, w_z_ref, w_xproj_ref, w_dt_ref, a_log_ref, w_out_ref, out_grad_ref,
    tok_s, og_s, end_s, sum_s, sems,
):
    copies = fetch(
        (
            (tokens_hbm, tokens_ref),
            (w_in_hbm.at[:, 0:C], w_x_ref),
            (w_xproj_hbm, w_xproj_ref),
            (w_dt_hbm, w_dt_ref),
            (a_log_hbm, a_log_ref),
            (w_in_hbm.at[:, C : 2 * C], w_z_ref),
            (out_grad_hbm, out_grad_ref),
            (w_out_hbm, w_out_ref),
        ),
        sems,
    )
    tok_s[...] = jnp.zeros_like(tok_s)
    og_s[...] = jnp.zeros_like(og_s)
    copies[0].wait()
    for i in range(T):
        tok_s[i, 0:T, :] = tokens_ref[i]
    tok = tok_s[...].reshape(CELLS, C)
    copies[1].wait()
    x_pre = jnp.dot(tok, w_x_ref[...], preferred_element_type=F32)
    x_pre_ref[...] = x_pre
    x_act = (x_pre * jax.nn.sigmoid(x_pre)).astype(BF16)
    copies[2].wait()
    dt_low = nt(x_act, w_xproj_ref[...])[:, 0:48].astype(BF16)
    x_dbl_t = nt(w_xproj_ref[...], x_act)
    for i in range(T):
        for j in range(T):
            cell = PAD * i + j
            b_ref[cell] = jnp.broadcast_to(x_dbl_t[48:64, cell : cell + 1], (N, 128))
            c_ref[cell] = jnp.broadcast_to(x_dbl_t[64:80, cell : cell + 1], (N, 128))
    copies[3].wait()
    dt_pre = jnp.dot(dt_low, w_dt_ref[...], preferred_element_type=F32) + dt_bias_ref[...]
    dt_pre_ref[...] = dt_pre
    step = jnp.maximum(dt_pre, 0.0) + jnp.log1p(jnp.exp(-jnp.abs(dt_pre)))
    step_ref[...] = step.reshape(T, PAD, C)
    x_full = x_act.astype(F32)
    x_ref[...] = x_full
    u_ref[...] = (step * x_full).reshape(T, PAD, C)
    copies[4].wait()
    rates_ref[...] = -jnp.exp(a_log_ref[...]) * LOG2E
    copies[5].wait()
    z_pre = jnp.dot(tok, w_z_ref[...], preferred_element_type=F32)
    z_pre_ref[...] = z_pre
    copies[6].wait()
    for i in range(T):
        og_s[i, 0:T, :] = out_grad_ref[i]
    copies[7].wait()
    gated = nt(og_s[...].reshape(CELLS, C), w_out_ref[...])
    gated_ref[...] = gated
    grad_ref[...] = (gated * (z_pre * jax.nn.sigmoid(z_pre))).reshape(T, PAD, C)
    term_ref[...] = jnp.zeros_like(term_ref)

    def one_row(back, carry):
        i = T - 1 - back
        row = [jnp.zeros((N, 128), F32) for _ in LANES]
        for j in range(T):
            b = b_ref[PAD * i + j]
            c = c_ref[PAD * i + j]
            for k, lanes in enumerate(LANES):
                decay = jnp.exp2(rates_ref[:, lanes] * step_ref[i, j : j + 1, lanes])
                row[k] = decay * row[k] + b * u_ref[i, j : j + 1, lanes]
                term_ref[j, :, lanes] = decay * (
                    c * grad_ref[i, j : j + 1, lanes] + term_ref[j, :, lanes]
                )
        for k, lanes in enumerate(LANES):
            end_s[i, :, lanes] = row[k]
        return carry

    lax.fori_loop(0, T, one_row, 0)
    for i in range(T):
        sum_s[i : i + 1, :] = jnp.sum(step_ref[i, 0:T, :], axis=0, keepdims=True)
    core = lax.axis_index("col") % 2
    for ref, half in ((own_ref, core), (other_ref, 1 - core)):
        pack_half(one_half(ref), 0, end_s, half)
        pack_sums(one_half(ref), 72, sum_s, half)


def chip_decay(core, rates_ref, part, group, t, k):
    states = 8 * ((3 * group + t) % 2)
    u = (3 * group + t) // 2 - 3 * group // 2
    rate = rates_ref[states : states + 8, half_lanes(core, k)]
    return jnp.exp2(rate * part[72 + 3 * u + k : 73 + 3 * u + k, :])


def combine_kernel(reverse, own_ref, got_ref, own_sums_ref, got_sums_ref, rates_ref, out_ref):
    core = lax.axis_index("col") % 2
    own_first = core == (1 if reverse else 0)
    for group in range(8):
        own, got = own_ref[group], got_ref[group]
        own_sums, got_sums = own_sums_ref[group], got_sums_ref[group]
        early, late = jnp.where(own_first, own, got), jnp.where(own_first, got, own)
        late_sums = jnp.where(own_first, got_sums, own_sums)
        for t in range(3):
            for k in range(3):
                rows = slice(8 * (3 * t + k), 8 * (3 * t + k) + 8)
                decay = chip_decay(core, rates_ref, late_sums, group, t, k)
                out_ref[group, rows, :] = decay * early[rows] + late[rows]
        if not reverse:
            out_ref[group, 72:80, :] = own[72:80] + got[72:80]


def split_kernel(
    reverse, state_ref, own_ref, got_ref, own_sums_ref, got_sums_ref, rates_ref, keep_ref, send_ref
):
    core = lax.axis_index("col") % 2
    own_first = core == (1 if reverse else 0)
    for group in range(8):
        early = jnp.where(own_first, own_ref[group], got_ref[group])
        early_sums = jnp.where(own_first, own_sums_ref[group], got_sums_ref[group])
        for t in range(3):
            for k in range(3):
                rows = slice(8 * (3 * t + k), 8 * (3 * t + k) + 8)
                state = state_ref[group, rows, :]
                through = (
                    chip_decay(core, rates_ref, early_sums, group, t, k) * state + early[rows]
                )
                keep_ref[group, rows, :] = jnp.where(own_first, state, through)
                send_ref[group, rows, :] = jnp.where(own_first, through, state)


def prefix_kernel(axis, spans, sum_base, got_ref, sums_ref, rates_ref, out_ref):
    me = lax.axis_index(axis)
    group, half = me // 2, me % 2
    tiles = got_ref.shape[0]
    for t in range(3):
        states = pl.multiple_of(8 * ((3 * group + t) % 2), 8)
        later = (3 * group + t) // 2 > (3 * group) // 2
        for k in range(3):
            rate = rates_ref[pl.ds(states, 8), half_lanes(half, k)]
            for base, reverse in spans:
                state = jnp.zeros((8, 128), F32)
                rows = slice(base + 8 * (3 * t + k), base + 8 * (3 * t + k) + 8)
                for hop in range(tiles):
                    tile = tiles - 1 - hop if reverse else hop
                    out_ref[tile, rows, :] = state
                    total = jnp.where(
                        later,
                        sums_ref[tile, sum_base + 3 + k : sum_base + 4 + k, :],
                        sums_ref[tile, sum_base + k : sum_base + k + 1, :],
                    )
                    state = jnp.exp2(rate * total) * state + got_ref[tile, rows, :]


def forward_kernel(
    keep_ref, came_ref, rates_s, step_ref, u_ref, b_ref, term_ref, sent_ref, row_s, col_s, sum_s
):
    core = lax.axis_index("col") % 2
    unpack_half(row_s, one_half(keep_ref), 0, core)
    unpack_half(row_s, one_half(came_ref), 0, 1 - core)
    col_s[...] = jnp.zeros_like(col_s)

    def one_row(i, carry):
        row = [row_s[i, :, lanes] for lanes in LANES]
        for j in range(T):
            b = b_ref[PAD * i + j]
            for k, lanes in enumerate(LANES):
                decay = jnp.exp2(rates_s[:, lanes] * step_ref[i, j : j + 1, lanes])
                row[k] = decay * row[k] + b * u_ref[i, j : j + 1, lanes]
                col_s[j, :, lanes] = decay * col_s[j, :, lanes] + row[k]
        return carry

    lax.fori_loop(0, T, one_row, 0)
    total = step_ref[0]
    for i in range(1, T):
        total = total + step_ref[i]
    sum_s[...] = total
    for half, chunk_of in enumerate(both_halves(sent_ref)):
        pack_half(chunk_of, 0, col_s, half)
        pack_half(chunk_of, 72, term_ref, half)
        pack_sums(chunk_of, 144, sum_s, half)


def backward_kernel(
    col_got_ref, rates_s, step_ref, grad_ref, c_ref, own_ref, other_ref, term_s, end_s
):
    for half, chunk_of in enumerate(both_halves(col_got_ref)):
        unpack_half(term_s, chunk_of, 72, half)

    def one_row(back, carry):
        i = T - 1 - back
        row = [jnp.zeros((N, 128), F32) for _ in LANES]
        for j in reversed(range(T)):
            c = c_ref[PAD * i + j]
            for k, lanes in enumerate(LANES):
                decay = jnp.exp2(rates_s[:, lanes] * step_ref[i, j : j + 1, lanes])
                adjoint = c * grad_ref[i, j : j + 1, lanes] + term_s[j, :, lanes]
                term_s[j, :, lanes] = decay * adjoint
                row[k] = decay * (adjoint + row[k])
        for k, lanes in enumerate(LANES):
            end_s[i, :, lanes] = row[k]
        return carry

    lax.fori_loop(0, T, one_row, 0)
    core = lax.axis_index("col") % 2
    pack_half(one_half(own_ref), 0, end_s, core)
    pack_half(one_half(other_ref), 0, end_s, 1 - core)


def last_kernel(
    keep_ref, came_ref, col_got_ref, back_keep_ref, back_came_ref, x_pre_ref, z_pre_ref, dt_pre_ref, gated_ref, step_ref,
    u_ref, x_ref, grad_ref, b_ref, c_ref, rates_s, d_skip_ref, w_in_hbm, w_xproj_hbm, w_dt_hbm,
    w_out_hbm,
    layer_hbm, token_hbm,
    w_in_ref, w_xproj_ref, w_dt_ref, w_out_ref, layer_ref, token_ref,
    row_s, col_s, full_keep, row_keep, scan_s, step_sum_s, x_sum_s, b_part, c_part, w_dt_s, sems,
):
    copies = fetch(
        (
            (w_out_hbm, w_out_ref),
            (w_dt_hbm, w_dt_ref),
            (w_xproj_hbm, w_xproj_ref),
            (w_in_hbm, w_in_ref),
        ),
        sems,
    )
    core = lax.axis_index("col") % 2
    unpack_half(row_s, one_half(keep_ref), 0, core)
    unpack_half(row_s, one_half(came_ref), 0, 1 - core)
    for half, chunk_of in enumerate(both_halves(col_got_ref)):
        unpack_half(col_s, chunk_of, 0, half)
    for ref in (scan_s, step_sum_s, x_sum_s, b_part, c_part):
        ref[...] = jnp.zeros_like(ref)

    def down_row(i, carry):
        row = [row_s[i, :, lanes] for lanes in LANES]
        for j in range(T):
            cell = PAD * i + j
            b = b_ref[cell]
            c = c_ref[cell]
            part = jnp.zeros((N, 128), F32)
            for k, lanes in enumerate(LANES):
                decay = jnp.exp2(rates_s[:, lanes] * step_ref[i, j : j + 1, lanes])
                row_old = decay * row[k]
                row[k] = row_old + b * u_ref[i, j : j + 1, lanes]
                full_old = decay * col_s[j, :, lanes]
                full = full_old + row[k]
                col_s[j, :, lanes] = full
                row_keep[T * i + j, :, lanes] = row_old
                full_keep[T * i + j, :, lanes] = full_old
                scan_s[i, j : j + 1, lanes] = jnp.sum(c * full, axis=0, keepdims=True)
                part = part + full * grad_ref[i, j : j + 1, lanes]
            c_part[cell] = part
        return carry

    lax.fori_loop(0, T, down_row, 0)
    x = x_ref[...]
    z_pre = z_pre_ref[...]
    skip = d_skip_ref[...]
    scan_out = scan_s[...].reshape(CELLS, C) + skip * x
    z_sig = jax.nn.sigmoid(z_pre)
    gated_out = (scan_out * (z_pre * z_sig)).astype(BF16)
    copies[0].wait()
    layer = jnp.dot(gated_out, w_out_ref[...], preferred_element_type=F32).astype(BF16)
    for i in range(T):
        layer_ref[i] = layer[PAD * i : PAD * i + T, :]
    layer_copy = pltpu.make_async_copy(layer_ref, layer_hbm, sems.at[4])
    layer_copy.start()
    scan_s[...] = (gated_ref[...] * scan_out * (z_sig * (1.0 + z_pre * (1.0 - z_sig)))).reshape(
        T, PAD, C
    )
    for half, chunk_of in enumerate(both_halves(col_got_ref)):
        unpack_half(col_s, chunk_of, 72, half)
    unpack_half(row_s, one_half(back_keep_ref), 0, core)
    unpack_half(row_s, one_half(back_came_ref), 0, 1 - core)

    def up_row(back, carry):
        i = T - 1 - back
        row = [row_s[i, :, lanes] for lanes in LANES]
        for j in reversed(range(T)):
            cell = PAD * i + j
            b = b_ref[cell]
            c = c_ref[cell]
            part = jnp.zeros((N, 128), F32)
            for k, lanes in enumerate(LANES):
                decay = jnp.exp2(rates_s[:, lanes] * step_ref[i, j : j + 1, lanes])
                col_adjoint = c * grad_ref[i, j : j + 1, lanes] + col_s[j, :, lanes]
                col_s[j, :, lanes] = decay * col_adjoint
                row_adjoint = col_adjoint + row[k]
                row[k] = decay * row_adjoint
                decay_grad = (
                    col_adjoint * full_keep[T * i + j, :, lanes] + row_adjoint * row_keep[T * i + j, :, lanes]
                )
                step_sum_s[i, j : j + 1, lanes] = jnp.sum(
                    decay_grad * rates_s[:, lanes], axis=0, keepdims=True
                )
                x_sum_s[i, j : j + 1, lanes] = jnp.sum(row_adjoint * b, axis=0, keepdims=True)
                part = part + row_adjoint * u_ref[i, j : j + 1, lanes]
            b_part[cell] = part
        return carry

    lax.fori_loop(0, T, up_row, 0)

    x = x_ref[...]
    x_pre = x_pre_ref[...]
    step = step_ref[...].reshape(CELLS, C)
    grad = grad_ref[...].reshape(CELLS, C)
    x_sum = x_sum_s[...].reshape(CELLS, C)
    step_grad = step_sum_s[...].reshape(CELLS, C) * (1.0 / LOG2E) + x_sum * x
    pre_grad = (step_grad * jax.nn.sigmoid(dt_pre_ref[...])).astype(BF16)
    copies[1].wait()
    w_dt_s[...] = jnp.zeros_like(w_dt_s)
    w_dt_s[0:48, :] = w_dt_ref[...]
    low = nt(pre_grad, w_dt_s[...])
    rows = lax.broadcasted_iota(jnp.int32, (CELLS * N, 80), 0)
    cols = lax.broadcasted_iota(jnp.int32, (CELLS * N, 80), 1)
    state = rows % N
    b_sum = jnp.sum(b_part[...].reshape(CELLS * N, 128), axis=1, keepdims=True)
    c_sum = jnp.sum(c_part[...].reshape(CELLS * N, 128), axis=1, keepdims=True)
    placed = jnp.where(cols == state + 48, b_sum, jnp.where(cols == state + 64, c_sum, 0.0))
    owner = lax.broadcasted_iota(jnp.int32, (CELLS, CELLS * N), 1) // N
    cell = lax.broadcasted_iota(jnp.int32, (CELLS, CELLS * N), 0)
    choose = (owner == cell).astype(F32).astype(BF16)
    dbl = (low + jnp.dot(choose, placed.astype(BF16), preferred_element_type=F32)).astype(BF16)
    copies[2].wait()
    x_grad = (
        x_sum * step
        + grad * d_skip_ref[...]
        + jnp.dot(dbl, w_xproj_ref[...], preferred_element_type=F32)
    )
    x_sig = jax.nn.sigmoid(x_pre)
    x_part = (x_grad * (x_sig * (1.0 + x_pre * (1.0 - x_sig)))).astype(BF16)
    z_part = scan_s[...].reshape(CELLS, C).astype(BF16)
    copies[3].wait()
    token = (nt(x_part, w_in_ref[:, 0:C]) + nt(z_part, w_in_ref[:, C : 2 * C])).astype(BF16)
    for i in range(T):
        token_ref[i] = token[PAD * i : PAD * i + T, :]
    token_copy = pltpu.make_async_copy(token_ref, token_hbm, sems.at[5])
    token_copy.start()
    layer_copy.wait()
    token_copy.wait()


IN_VMEM = pl.BlockSpec(memory_space=pltpu.VMEM)
IN_HBM = pl.BlockSpec(memory_space=pltpu.HBM)


def call(kernel, out_shape, scratch, name, limit, *args, fetched=(), out_spec=IN_VMEM):
    many = isinstance(out_shape, tuple)
    return pl.pallas_call(
        kernel,
        out_shape=out_shape,
        in_specs=[IN_HBM if k in fetched else IN_VMEM for k in range(len(args))],
        out_specs=tuple(out_spec for _ in out_shape) if many else out_spec,
        scratch_shapes=scratch,
        name=name,
        compiler_params=pltpu.CompilerParams(vmem_limit_bytes=limit * 1024 * 1024),
    )(*args)


def f32(*shape):
    return jax.ShapeDtypeStruct(shape, F32)


def vmem(*shape):
    return pltpu.VMEM(shape, F32)


def prefix(axis, spans, sum_base, rows, got, sums, rates):
    def kernel(got_ref, sums_ref, rates_ref, out_ref):
        prefix_kernel(axis, spans, sum_base, got_ref, sums_ref, rates_ref, out_ref)

    out = f32(got.shape[0], rows, 128)
    return call(kernel, out, (), "prefix_" + axis, 4, got, sums, rates)


def swap(sent, axis, groups=None):
    return lax.all_to_all(sent, axis, 0, 0, tiled=True, axis_index_groups=groups)


def row_scan(own, other, sums, rates, reverse):
    partner = [(place, place ^ 1) for place in range(16)]
    same_core = [[2 * chip + core for chip in range(8)] for core in range(2)]
    got = lax.ppermute(other, "col", partner)
    if sums is None:
        sums = (own, got)

    def combine(*refs):
        combine_kernel(reverse, *refs)

    def split(*refs):
        split_kernel(reverse, *refs)

    chip = call(
        combine, f32(8, own.shape[1], 128), (), "combine", 6, own, got, *sums[:2], rates
    )
    chips = swap(chip, "col", same_core)
    chip_sums = chips if len(sums) == 2 else sums[2]
    state = swap(
        prefix("col", ((0, reverse),), 72, 72, chips, chip_sums, rates), "col", same_core
    )
    half = f32(8, 72, 128)
    keep, send = call(split, (half, half), (), "split", 6, state, own, got, *sums[:2], rates)
    return keep, lax.ppermute(send, "col", partner), (*sums[:2], chip_sums)


def body(tokens, w_in, w_xproj, w_dt, dt_bias, a_log, d_skip, w_out, out_grad):
    edge, wide = vmem(T, N, C), vmem(T, PAD, C)
    flat, grid, spread = f32(CELLS, C), f32(T, PAD, C), f32(CELLS, N, 128)
    kept, sums = vmem(T * T, N, C), vmem(PAD, C)
    padded, cells = pltpu.VMEM((T, PAD, C), BF16), pltpu.VMEM((T, T, C), BF16)
    square, narrow = pltpu.VMEM((C, C), BF16), pltpu.VMEM((80, C), BF16)
    low_rank = pltpu.VMEM((48, C), BF16)
    w_xproj = w_xproj.T
    x_pre, z_pre, dt_pre, gated, step, u, x, grad, b, c, term, rates, own, other = call(
        first_kernel,
        (
            flat, flat, flat, flat, grid, grid, flat, grid, spread, spread, f32(T, N, C),
            f32(N, C), f32(8, 80, 128), f32(8, 80, 128),
        ),
        (
            cells, square, square, narrow, low_rank, vmem(N, C), square, cells,
            padded, padded, edge, sums, pltpu.SemaphoreType.DMA((8,)),
        ),
        "first", 54,
        tokens, w_in, w_xproj, w_dt, a_log, w_out, out_grad, dt_bias,
        fetched=range(7),
    )
    keep, came, chip_sums = row_scan(own, other, None, rates, False)
    col_sent = call(
        forward_kernel, f32(16, 152, 128), (edge, edge, sums), "forward", 6,
        keep, came, rates, step, u, b, term,
    )
    col_all = swap(col_sent, "row")
    col_got = swap(
        prefix("row", ((0, False), (72, True)), 144, 144, col_all, col_all, rates), "row"
    )
    back_half = f32(8, 72, 128)
    back_own, back_other = call(
        backward_kernel, (back_half, back_half), (edge, edge), "backward", 6,
        col_got, rates, step, grad, c,
    )
    back_keep, back_came, chip_sums = row_scan(back_own, back_other, chip_sums, rates, True)
    out = jax.ShapeDtypeStruct((T, T, C), BF16)
    return call(
        last_kernel,
        (out, out),
        (
            pltpu.VMEM((C, 2 * C), BF16), narrow, low_rank, square, cells, cells,
            edge, edge, kept, kept, wide, wide, wide,
            vmem(CELLS, N, 128), vmem(CELLS, N, 128), narrow, pltpu.SemaphoreType.DMA((6,)),
        ),
        "last", 42,
        keep, came, col_got, back_keep, back_came, x_pre, z_pre, dt_pre, gated, step, u, x, grad, b, c, rates,
        d_skip, w_in, w_xproj, w_dt, w_out,
        fetched=range(17, 21), out_spec=IN_HBM,
    )


def solution(mesh):
    return jax.shard_map(
        body,
        mesh=mesh,
        in_specs=(P("row", "col", None), P(), P(), P(), P(), P(), P(), P(), P("row", "col", None)),
        out_specs=(P("row", "col", None), P("row", "col", None)),
        check_vma=False,
    )
```

```python
import jax
import jax.numpy as jnp
from jax import lax
from jax.experimental import pallas as pl
from jax.experimental.pallas import tpu as pltpu
from jax.sharding import PartitionSpec as P

LOG2E = 1.4426950408889634
T = 12
PAD = 16
CELLS = T * PAD
N = 16
C = 768
HALF = 384
LANES = [slice(128 * k, 128 * k + 128) for k in range(C // 128)]
F32, BF16 = jnp.float32, jnp.bfloat16


def nt(left, right):
    return lax.dot_general(left, right, (((1,), (1,)), ((), ())), preferred_element_type=F32)


def pieces():
    for i in range(T):
        for h in range(2):
            q = 2 * i + h
            for k in range(3):
                yield i, slice(8 * h, 8 * h + 8), k, q // 3, 8 * (3 * (q % 3) + k)


def half_lanes(half, k):
    if isinstance(half, int):
        return slice(HALF * half + 128 * k, HALF * half + 128 * k + 128)
    return pl.ds(pl.multiple_of(HALF * half + 128 * k, 128), 128)


def pack_half(chunk_of, base, edge_ref, half):
    for i, states, k, group, row in pieces():
        chunk_of(group)[base + row : base + row + 8, :] = edge_ref[i, states, half_lanes(half, k)]


def unpack_half(edge_ref, chunk_of, base, half):
    for i, states, k, group, row in pieces():
        edge_ref[i, states, half_lanes(half, k)] = chunk_of(group)[base + row : base + row + 8, :]


def pack_sums(chunk_of, base, sum_ref, half):
    for group in range(8):
        rows = [
            sum_ref[pl.ds(3 * group // 2 + u, 1), half_lanes(half, k)]
            for u in range(2)
            for k in range(3)
        ]
        chunk_of(group)[base : base + 8, :] = jnp.concatenate(
            rows + [jnp.zeros((2, 128), F32)], axis=0
        )


def both_halves(ref):
    return [(lambda group, half=half: ref.at[2 * group + half]) for half in range(2)]


def one_half(ref):
    return lambda group: ref.at[group]


def fetch(pairs, sems, now=None):
    copies = [pltpu.make_async_copy(src, dst, sems.at[k]) for k, (src, dst) in enumerate(pairs)]
    for copy in copies[:now]:
        copy.start()
    return copies


def first_kernel(
    tokens_hbm, w_in_hbm, w_xproj_hbm, w_dt_hbm, a_log_hbm, w_out_hbm, out_grad_hbm, dt_bias_ref,
    x_pre_hbm, z_pre_hbm, dt_pre_hbm, gated_hbm, step_hbm, u_hbm, x_hbm, grad_hbm, b_hbm, c_hbm,
    term_ref, rates_ref, own_ref, other_ref,
    x_pre_ref, z_pre_ref, dt_pre_ref, gated_ref, step_ref, u_ref, x_ref, grad_ref, b_ref, c_ref,
    tokens_ref, w_x_ref, w_z_ref, w_xproj_ref, w_dt_ref, a_log_ref, w_out_ref, out_grad_ref,
    tok_s, og_s, end_s, sum_s, sems, out_sems,
):
    leaving = []

    def leave(src, dst):
        copy = pltpu.make_async_copy(src, dst, out_sems.at[len(leaving)])
        copy.start()
        leaving.append(copy)

    copies = fetch(
        (
            (tokens_hbm, tokens_ref),
            (w_in_hbm.at[:, 0:C], w_x_ref),
            (w_xproj_hbm, w_xproj_ref),
            (w_dt_hbm, w_dt_ref),
            (a_log_hbm, a_log_ref),
            (w_in_hbm.at[:, C : 2 * C], w_z_ref),
            (out_grad_hbm, out_grad_ref),
            (w_out_hbm, w_out_ref),
        ),
        sems,
        5,
    )
    tok_s[...] = jnp.zeros_like(tok_s)
    og_s[...] = jnp.zeros_like(og_s)
    copies[0].wait()
    for i in range(T):
        tok_s[i, 0:T, :] = tokens_ref[i]
    tok = tok_s[...].reshape(CELLS, C)
    copies[1].wait()
    for copy in copies[5:]:
        copy.start()
    x_pre = jnp.dot(tok, w_x_ref[...], preferred_element_type=F32)
    x_pre_ref[...] = x_pre
    x_act = (x_pre * jax.nn.sigmoid(x_pre)).astype(BF16)
    copies[2].wait()
    leave(x_pre_ref, x_pre_hbm)
    dt_low = nt(x_act, w_xproj_ref[...])[:, 0:48].astype(BF16)
    x_dbl_t = nt(w_xproj_ref[...], x_act)
    for i in range(T):
        for j in range(T):
            cell = PAD * i + j
            b_ref[cell] = jnp.broadcast_to(x_dbl_t[48:64, cell : cell + 1], (N, 128))
            c_ref[cell] = jnp.broadcast_to(x_dbl_t[64:80, cell : cell + 1], (N, 128))
    leave(b_ref, b_hbm)
    leave(c_ref, c_hbm)
    copies[3].wait()
    dt_pre = jnp.dot(dt_low, w_dt_ref[...], preferred_element_type=F32) + dt_bias_ref[...]
    dt_pre_ref[...] = dt_pre
    step = jnp.maximum(dt_pre, 0.0) + jnp.log1p(jnp.exp(-jnp.abs(dt_pre)))
    step_ref[...] = step.reshape(T, PAD, C)
    x_full = x_act.astype(F32)
    x_ref[...] = x_full
    u_ref[...] = (step * x_full).reshape(T, PAD, C)
    leave(dt_pre_ref, dt_pre_hbm)
    leave(step_ref, step_hbm)
    leave(x_ref, x_hbm)
    leave(u_ref, u_hbm)
    copies[4].wait()
    rates_ref[...] = -jnp.exp(a_log_ref[...]) * LOG2E
    copies[5].wait()
    z_pre = jnp.dot(tok, w_z_ref[...], preferred_element_type=F32)
    z_pre_ref[...] = z_pre
    leave(z_pre_ref, z_pre_hbm)
    copies[6].wait()
    for i in range(T):
        og_s[i, 0:T, :] = out_grad_ref[i]
    copies[7].wait()
    gated = nt(og_s[...].reshape(CELLS, C), w_out_ref[...])
    gated_ref[...] = gated
    grad_ref[...] = (gated * (z_pre * jax.nn.sigmoid(z_pre))).reshape(T, PAD, C)
    leave(gated_ref, gated_hbm)
    leave(grad_ref, grad_hbm)
    term_ref[...] = jnp.zeros_like(term_ref)

    def one_row(back, carry):
        i = T - 1 - back
        row = [jnp.zeros((N, 128), F32) for _ in LANES]
        for j in range(T):
            b = b_ref[PAD * i + j]
            c = c_ref[PAD * i + j]
            for k, lanes in enumerate(LANES):
                decay = jnp.exp2(rates_ref[:, lanes] * step_ref[i, j : j + 1, lanes])
                row[k] = decay * row[k] + b * u_ref[i, j : j + 1, lanes]
                term_ref[j, :, lanes] = decay * (
                    c * grad_ref[i, j : j + 1, lanes] + term_ref[j, :, lanes]
                )
        for k, lanes in enumerate(LANES):
            end_s[i, :, lanes] = row[k]
        return carry

    lax.fori_loop(0, T, one_row, 0)
    for i in range(T):
        sum_s[i : i + 1, :] = jnp.sum(step_ref[i, 0:T, :], axis=0, keepdims=True)
    core = lax.axis_index("col") % 2
    for ref, half in ((own_ref, core), (other_ref, 1 - core)):
        pack_half(one_half(ref), 0, end_s, half)
        pack_sums(one_half(ref), 72, sum_s, half)
    for copy in leaving:
        copy.wait()


def chip_decay(core, rates_ref, part, group, t, k):
    states = 8 * ((3 * group + t) % 2)
    u = (3 * group + t) // 2 - 3 * group // 2
    rate = rates_ref[states : states + 8, half_lanes(core, k)]
    return jnp.exp2(rate * part[72 + 3 * u + k : 73 + 3 * u + k, :])


def combine_kernel(reverse, own_ref, got_ref, own_sums_ref, got_sums_ref, rates_ref, out_ref):
    core = lax.axis_index("col") % 2
    own_first = core == (1 if reverse else 0)
    for group in range(8):
        own, got = own_ref[group], got_ref[group]
        own_sums, got_sums = own_sums_ref[group], got_sums_ref[group]
        early, late = jnp.where(own_first, own, got), jnp.where(own_first, got, own)
        late_sums = jnp.where(own_first, got_sums, own_sums)
        for t in range(3):
            for k in range(3):
                rows = slice(8 * (3 * t + k), 8 * (3 * t + k) + 8)
                decay = chip_decay(core, rates_ref, late_sums, group, t, k)
                out_ref[group, rows, :] = decay * early[rows] + late[rows]
        if not reverse:
            out_ref[group, 72:80, :] = own[72:80] + got[72:80]


def split_kernel(
    reverse, state_ref, own_ref, got_ref, own_sums_ref, got_sums_ref, rates_ref, keep_ref, send_ref
):
    core = lax.axis_index("col") % 2
    own_first = core == (1 if reverse else 0)
    for group in range(8):
        early = jnp.where(own_first, own_ref[group], got_ref[group])
        early_sums = jnp.where(own_first, own_sums_ref[group], got_sums_ref[group])
        for t in range(3):
            for k in range(3):
                rows = slice(8 * (3 * t + k), 8 * (3 * t + k) + 8)
                state = state_ref[group, rows, :]
                through = (
                    chip_decay(core, rates_ref, early_sums, group, t, k) * state + early[rows]
                )
                keep_ref[group, rows, :] = jnp.where(own_first, state, through)
                send_ref[group, rows, :] = jnp.where(own_first, through, state)


def prefix_kernel(axis, spans, sum_base, got_ref, sums_ref, rates_ref, out_ref):
    me = lax.axis_index(axis)
    group, half = me // 2, me % 2
    tiles = got_ref.shape[0]
    for t in range(3):
        states = pl.multiple_of(8 * ((3 * group + t) % 2), 8)
        later = (3 * group + t) // 2 > (3 * group) // 2
        for k in range(3):
            rate = rates_ref[pl.ds(states, 8), half_lanes(half, k)]
            for base, reverse in spans:
                state = jnp.zeros((8, 128), F32)
                rows = slice(base + 8 * (3 * t + k), base + 8 * (3 * t + k) + 8)
                for hop in range(tiles):
                    tile = tiles - 1 - hop if reverse else hop
                    out_ref[tile, rows, :] = state
                    total = jnp.where(
                        later,
                        sums_ref[tile, sum_base + 3 + k : sum_base + 4 + k, :],
                        sums_ref[tile, sum_base + k : sum_base + k + 1, :],
                    )
                    state = jnp.exp2(rate * total) * state + got_ref[tile, rows, :]


def forward_kernel(
    keep_ref, came_ref, rates_s, step_ref, u_ref, b_ref, term_ref, sent_ref, row_s, col_s, sum_s
):
    core = lax.axis_index("col") % 2
    unpack_half(row_s, one_half(keep_ref), 0, core)
    unpack_half(row_s, one_half(came_ref), 0, 1 - core)
    col_s[...] = jnp.zeros_like(col_s)

    def one_row(i, carry):
        row = [row_s[i, :, lanes] for lanes in LANES]
        for j in range(T):
            b = b_ref[PAD * i + j]
            for k, lanes in enumerate(LANES):
                decay = jnp.exp2(rates_s[:, lanes] * step_ref[i, j : j + 1, lanes])
                row[k] = decay * row[k] + b * u_ref[i, j : j + 1, lanes]
                col_s[j, :, lanes] = decay * col_s[j, :, lanes] + row[k]
        return carry

    lax.fori_loop(0, T, one_row, 0)
    total = step_ref[0]
    for i in range(1, T):
        total = total + step_ref[i]
    sum_s[...] = total
    for half, chunk_of in enumerate(both_halves(sent_ref)):
        pack_half(chunk_of, 0, col_s, half)
        pack_half(chunk_of, 72, term_ref, half)
        pack_sums(chunk_of, 144, sum_s, half)


def backward_kernel(
    col_got_ref, rates_s, step_ref, grad_ref, c_ref, own_ref, other_ref, term_s, end_s
):
    for half, chunk_of in enumerate(both_halves(col_got_ref)):
        unpack_half(term_s, chunk_of, 72, half)

    def one_row(back, carry):
        i = T - 1 - back
        row = [jnp.zeros((N, 128), F32) for _ in LANES]
        for j in reversed(range(T)):
            c = c_ref[PAD * i + j]
            for k, lanes in enumerate(LANES):
                decay = jnp.exp2(rates_s[:, lanes] * step_ref[i, j : j + 1, lanes])
                adjoint = c * grad_ref[i, j : j + 1, lanes] + term_s[j, :, lanes]
                term_s[j, :, lanes] = decay * adjoint
                row[k] = decay * (adjoint + row[k])
        for k, lanes in enumerate(LANES):
            end_s[i, :, lanes] = row[k]
        return carry

    lax.fori_loop(0, T, one_row, 0)
    core = lax.axis_index("col") % 2
    pack_half(one_half(own_ref), 0, end_s, core)
    pack_half(one_half(other_ref), 0, end_s, 1 - core)


def put_part(part_ref, i, j, k, values):
    rows = pl.ds(pl.multiple_of(8 * (PAD * i + j), 8), 8)
    part_ref[k, rows, :] = values[0:8] + values[8:16]


def add_parts(sum_ref, part_ref, i, turns=range(T)):
    for turn in turns:
        j, k = 8 * (turn // 6), turn % 6
        base = 8 * (PAD * i + j)
        total = part_ref[k, pl.ds(base, 8, stride=8), :]
        for r in range(1, 8):
            total = total + part_ref[k, pl.ds(base + r, 8, stride=8), :]
        sum_ref[i, j : j + 8, LANES[k]] = total


def last_kernel(
    keep_ref, came_ref, col_got_ref, back_keep_ref, back_came_ref, x_pre_ref, z_pre_ref, dt_pre_ref, gated_ref, step_ref,
    u_ref, x_ref, grad_ref, b_ref, c_ref, rates_s, d_skip_ref, w_in_hbm, w_xproj_hbm, w_dt_hbm,
    w_out_hbm,
    layer_hbm, token_hbm,
    w_in_ref, w_xproj_ref, w_dt_ref, w_out_ref, layer_ref, token_ref,
    row_s, col_s, full_keep, row_keep, scan_s, step_sum_s, x_sum_s, b_part, c_part, part_a, part_b, w_dt_s, act_s,
    z_part_s, dbl_s, sems,
):
    copies = fetch(
        (
            (w_out_hbm, w_out_ref),
            (w_dt_hbm, w_dt_ref),
            (w_xproj_hbm, w_xproj_ref),
            (w_in_hbm, w_in_ref),
        ),
        sems,
    )
    core = lax.axis_index("col") % 2
    unpack_half(row_s, one_half(keep_ref), 0, core)
    unpack_half(row_s, one_half(came_ref), 0, 1 - core)
    for half, chunk_of in enumerate(both_halves(col_got_ref)):
        unpack_half(col_s, chunk_of, 0, half)
    for ref in (b_part, c_part):
        ref[...] = jnp.zeros_like(ref)

    def down_row(i, carry):
        before = jnp.maximum(i - 1, 0)
        row = [row_s[i, :, lanes] for lanes in LANES]
        for j in range(T):
            cell = PAD * i + j
            b = b_ref[cell]
            c = c_ref[cell]
            part = jnp.zeros((N, 128), F32)
            for k, lanes in enumerate(LANES):
                decay = jnp.exp2(rates_s[:, lanes] * step_ref[i, j : j + 1, lanes])
                row_old = decay * row[k]
                row[k] = row_old + b * u_ref[i, j : j + 1, lanes]
                full_old = decay * col_s[j, :, lanes]
                full = full_old + row[k]
                col_s[j, :, lanes] = full
                row_keep[T * i + j, :, lanes] = row_old
                full_keep[T * i + j, :, lanes] = full_old
                put_part(part_a, i, j, k, c * full)
                part = part + full * grad_ref[i, j : j + 1, lanes]
            c_part[cell] = part
            add_parts(scan_s, part_a, before, (j,))
        return carry

    lax.fori_loop(0, T, down_row, 0)
    add_parts(scan_s, part_a, T - 1)
    skip = d_skip_ref[...]
    for i in range(T):
        rows = slice(PAD * i, PAD * i + PAD)
        z_pre = z_pre_ref[rows, :]
        scan_out = scan_s[i] + skip * x_ref[rows, :]
        z_sig = jax.nn.sigmoid(z_pre)
        act_s[rows, :] = (scan_out * (z_pre * z_sig)).astype(BF16)
        z_part_s[rows, :] = (
            gated_ref[rows, :] * scan_out * (z_sig * (1.0 + z_pre * (1.0 - z_sig)))
        ).astype(BF16)
    copies[0].wait()
    layer = jnp.dot(act_s[...], w_out_ref[...], preferred_element_type=F32).astype(BF16)
    for i in range(T):
        layer_ref[i] = layer[PAD * i : PAD * i + T, :]
    layer_copy = pltpu.make_async_copy(layer_ref, layer_hbm, sems.at[4])
    layer_copy.start()
    for half, chunk_of in enumerate(both_halves(col_got_ref)):
        unpack_half(col_s, chunk_of, 72, half)
    unpack_half(row_s, one_half(back_keep_ref), 0, core)
    unpack_half(row_s, one_half(back_came_ref), 0, 1 - core)

    def up_row(back, carry):
        i = T - 1 - back
        before = jnp.minimum(i + 1, T - 1)
        row = [row_s[i, :, lanes] for lanes in LANES]
        for j in reversed(range(T)):
            cell = PAD * i + j
            b = b_ref[cell]
            c = c_ref[cell]
            part = jnp.zeros((N, 128), F32)
            for k, lanes in enumerate(LANES):
                decay = jnp.exp2(rates_s[:, lanes] * step_ref[i, j : j + 1, lanes])
                col_adjoint = c * grad_ref[i, j : j + 1, lanes] + col_s[j, :, lanes]
                col_s[j, :, lanes] = decay * col_adjoint
                row_adjoint = col_adjoint + row[k]
                row[k] = decay * row_adjoint
                decay_grad = (
                    col_adjoint * full_keep[T * i + j, :, lanes] + row_adjoint * row_keep[T * i + j, :, lanes]
                )
                put_part(part_a, i, j, k, decay_grad * rates_s[:, lanes])
                put_part(part_b, i, j, k, row_adjoint * b)
                part = part + row_adjoint * u_ref[i, j : j + 1, lanes]
            b_part[cell] = part
            add_parts(step_sum_s, part_a, before, (j,))
            add_parts(x_sum_s, part_b, before, (j,))
        return carry

    lax.fori_loop(0, T, up_row, 0)
    add_parts(step_sum_s, part_a, 0)
    add_parts(x_sum_s, part_b, 0)

    state = lax.broadcasted_iota(jnp.int32, (PAD * N, 80), 0) % N
    col = lax.broadcasted_iota(jnp.int32, (PAD * N, 80), 1)
    at_b, at_c = col == state + 48, col == state + 64
    cell = lax.broadcasted_iota(jnp.int32, (PAD, PAD * N), 0)
    choose = lax.broadcasted_iota(jnp.int32, (PAD, PAD * N), 1) // N == cell
    choose = choose.astype(F32).astype(BF16)
    for i in range(T):
        rows = slice(PAD * i, PAD * i + PAD)
        step_grad = step_sum_s[i] * (1.0 / LOG2E) + x_sum_s[i] * x_ref[rows, :]
        act_s[rows, :] = (step_grad * jax.nn.sigmoid(dt_pre_ref[rows, :])).astype(BF16)
        b_sum = jnp.sum(b_part[rows].reshape(PAD * N, 128), axis=1, keepdims=True)
        c_sum = jnp.sum(c_part[rows].reshape(PAD * N, 128), axis=1, keepdims=True)
        placed = jnp.where(at_b, b_sum, jnp.where(at_c, c_sum, 0.0)).astype(BF16)
        dbl_s[rows, :] = jnp.dot(choose, placed, preferred_element_type=F32)
    copies[1].wait()
    w_dt_s[...] = jnp.zeros_like(w_dt_s)
    w_dt_s[0:48, :] = w_dt_ref[...]
    dbl = (nt(act_s[...], w_dt_s[...]) + dbl_s[...]).astype(BF16)
    copies[2].wait()
    step_sum_s[...] = jnp.dot(dbl, w_xproj_ref[...], preferred_element_type=F32).reshape(T, PAD, C)
    for i in range(T):
        rows = slice(PAD * i, PAD * i + PAD)
        x_pre = x_pre_ref[rows, :]
        x_grad = x_sum_s[i] * step_ref[i] + grad_ref[i] * skip + step_sum_s[i]
        x_sig = jax.nn.sigmoid(x_pre)
        act_s[rows, :] = (x_grad * (x_sig * (1.0 + x_pre * (1.0 - x_sig)))).astype(BF16)
    copies[3].wait()
    token = (nt(act_s[...], w_in_ref[:, 0:C]) + nt(z_part_s[...], w_in_ref[:, C : 2 * C])).astype(
        BF16
    )
    for i in range(T):
        token_ref[i] = token[PAD * i : PAD * i + T, :]
    token_copy = pltpu.make_async_copy(token_ref, token_hbm, sems.at[5])
    token_copy.start()
    layer_copy.wait()
    token_copy.wait()


IN_VMEM = pl.BlockSpec(memory_space=pltpu.VMEM)
IN_HBM = pl.BlockSpec(memory_space=pltpu.HBM)


def call(kernel, out_shape, scratch, name, limit, *args, fetched=(), sent=()):
    many = isinstance(out_shape, tuple)
    return pl.pallas_call(
        kernel,
        out_shape=out_shape,
        in_specs=[IN_HBM if k in fetched else IN_VMEM for k in range(len(args))],
        out_specs=tuple(IN_HBM if k in sent else IN_VMEM for k in range(len(out_shape)))
        if many
        else IN_VMEM,
        scratch_shapes=scratch,
        name=name,
        compiler_params=pltpu.CompilerParams(vmem_limit_bytes=limit * 1024 * 1024),
    )(*args)


def f32(*shape):
    return jax.ShapeDtypeStruct(shape, F32)


def vmem(*shape):
    return pltpu.VMEM(shape, F32)


def prefix(axis, spans, sum_base, rows, got, sums, rates):
    def kernel(got_ref, sums_ref, rates_ref, out_ref):
        prefix_kernel(axis, spans, sum_base, got_ref, sums_ref, rates_ref, out_ref)

    out = f32(got.shape[0], rows, 128)
    return call(kernel, out, (), "prefix_" + axis, 4, got, sums, rates)


def swap(sent, axis, groups=None):
    return lax.all_to_all(sent, axis, 0, 0, tiled=True, axis_index_groups=groups)


def row_scan(own, other, sums, rates, reverse):
    partner = [(place, place ^ 1) for place in range(16)]
    same_core = [[2 * chip + core for chip in range(8)] for core in range(2)]
    got = lax.ppermute(other, "col", partner)
    if sums is None:
        sums = (own, got)

    def combine(*refs):
        combine_kernel(reverse, *refs)

    def split(*refs):
        split_kernel(reverse, *refs)

    chip = call(
        combine, f32(8, own.shape[1], 128), (), "combine", 6, own, got, *sums[:2], rates
    )
    chips = swap(chip, "col", same_core)
    chip_sums = chips if len(sums) == 2 else sums[2]
    state = swap(
        prefix("col", ((0, reverse),), 72, 72, chips, chip_sums, rates), "col", same_core
    )
    half = f32(8, 72, 128)
    keep, send = call(split, (half, half), (), "split", 6, state, own, got, *sums[:2], rates)
    return keep, lax.ppermute(send, "col", partner), (*sums[:2], chip_sums)


def body(tokens, w_in, w_xproj, w_dt, dt_bias, a_log, d_skip, w_out, out_grad):
    edge, wide, dense = vmem(T, N, C), vmem(T, PAD, C), vmem(CELLS, C)
    flat, grid, spread = f32(CELLS, C), f32(T, PAD, C), f32(CELLS, N, 128)
    kept, sums, parts = vmem(T * T, N, C), vmem(PAD, C), vmem(C // 128, 8 * CELLS, 128)
    padded, cells = pltpu.VMEM((T, PAD, C), BF16), pltpu.VMEM((T, T, C), BF16)
    square, narrow = pltpu.VMEM((C, C), BF16), pltpu.VMEM((80, C), BF16)
    low_rank, half_width = pltpu.VMEM((48, C), BF16), pltpu.VMEM((CELLS, C), BF16)
    w_xproj = w_xproj.T
    x_pre, z_pre, dt_pre, gated, step, u, x, grad, b, c, term, rates, own, other = call(
        first_kernel,
        (
            flat, flat, flat, flat, grid, grid, flat, grid, spread, spread, f32(T, N, C),
            f32(N, C), f32(8, 80, 128), f32(8, 80, 128),
        ),
        (
            dense, dense, dense, dense, wide, wide, dense, wide, vmem(CELLS, N, 128),
            vmem(CELLS, N, 128), cells, square, square, narrow, low_rank, vmem(N, C), square, cells,
            padded, padded, edge, sums, pltpu.SemaphoreType.DMA((8,)),
            pltpu.SemaphoreType.DMA((10,)),
        ),
        "first", 54,
        tokens, w_in, w_xproj, w_dt, a_log, w_out, out_grad, dt_bias,
        fetched=range(7), sent=range(10),
    )
    keep, came, chip_sums = row_scan(own, other, None, rates, False)
    col_sent = call(
        forward_kernel, f32(16, 152, 128), (edge, edge, sums), "forward", 6,
        keep, came, rates, step, u, b, term,
    )
    col_all = swap(col_sent, "row")
    col_got = swap(
        prefix("row", ((0, False), (72, True)), 144, 144, col_all, col_all, rates), "row"
    )
    back_half = f32(8, 72, 128)
    back_own, back_other = call(
        backward_kernel, (back_half, back_half), (edge, edge), "backward", 6,
        col_got, rates, step, grad, c,
    )
    back_keep, back_came, chip_sums = row_scan(back_own, back_other, chip_sums, rates, True)
    out = jax.ShapeDtypeStruct((T, T, C), BF16)
    return call(
        last_kernel,
        (out, out),
        (
            pltpu.VMEM((C, 2 * C), BF16), narrow, low_rank, square, cells, cells,
            edge, edge, kept, kept, wide, wide, wide, vmem(CELLS, N, 128),
            vmem(CELLS, N, 128), parts, parts, narrow, half_width, half_width, vmem(CELLS, 80),
            pltpu.SemaphoreType.DMA((6,)),
        ),
        "last", 42,
        keep, came, col_got, back_keep, back_came, x_pre, z_pre, dt_pre, gated, step, u, x, grad, b, c, rates,
        d_skip, w_in, w_xproj, w_dt, w_out,
        fetched=range(17, 21), sent=range(2),
    )


def solution(mesh):
    return jax.shard_map(
        body,
        mesh=mesh,
        in_specs=(P("row", "col", None), P(), P(), P(), P(), P(), P(), P(), P("row", "col", None)),
        out_specs=(P("row", "col", None), P("row", "col", None)),
        check_vma=False,
    )
```

```python
import jax
import jax.numpy as jnp
from jax import lax
from jax.experimental import pallas as pl
from jax.experimental.pallas import tpu as pltpu
from jax.sharding import PartitionSpec as P

LOG2E = 1.4426950408889634
T = 12
PAD = 16
CELLS = T * PAD
N = 16
C = 768
HALF = 384
LANES = [slice(128 * k, 128 * k + 128) for k in range(C // 128)]
F32, BF16 = jnp.float32, jnp.bfloat16


def nt(left, right):
    return lax.dot_general(left, right, (((1,), (1,)), ((), ())), preferred_element_type=F32)


def pieces():
    for i in range(T):
        for h in range(2):
            q = 2 * i + h
            for k in range(3):
                yield i, slice(8 * h, 8 * h + 8), k, q // 3, 8 * (3 * (q % 3) + k)


def half_lanes(half, k):
    if isinstance(half, int):
        return slice(HALF * half + 128 * k, HALF * half + 128 * k + 128)
    return pl.ds(pl.multiple_of(HALF * half + 128 * k, 128), 128)


def pack_half(chunk_of, base, edge_ref, half):
    for i, states, k, group, row in pieces():
        chunk_of(group)[base + row : base + row + 8, :] = edge_ref[i, states, half_lanes(half, k)]


def unpack_half(edge_ref, chunk_of, base, half):
    for i, states, k, group, row in pieces():
        edge_ref[i, states, half_lanes(half, k)] = chunk_of(group)[base + row : base + row + 8, :]


def pack_sums(chunk_of, base, sum_ref, half):
    for group in range(8):
        rows = [
            sum_ref[pl.ds(3 * group // 2 + u, 1), half_lanes(half, k)]
            for u in range(2)
            for k in range(3)
        ]
        chunk_of(group)[base : base + 8, :] = jnp.concatenate(
            rows + [jnp.zeros((2, 128), F32)], axis=0
        )


def both_halves(ref):
    return [(lambda group, half=half: ref.at[2 * group + half]) for half in range(2)]


def one_half(ref):
    return lambda group: ref.at[group]


def fetch(pairs, sems, now=None):
    copies = [pltpu.make_async_copy(src, dst, sems.at[k]) for k, (src, dst) in enumerate(pairs)]
    for copy in copies[:now]:
        copy.start()
    return copies


def first_kernel(
    tokens_hbm, w_in_hbm, w_xproj_hbm, w_dt_hbm, a_log_hbm, w_out_hbm, out_grad_hbm, dt_bias_ref,
    x_pre_hbm, z_pre_hbm, dt_pre_hbm, gated_hbm, step_hbm, u_hbm, x_hbm, grad_hbm, b_hbm, c_hbm,
    term_hbm, rates_hbm, own_hbm, other_hbm,
    x_pre_ref, z_pre_ref, dt_pre_ref, gated_ref, step_ref, u_ref, x_ref, grad_ref, b_ref, c_ref,
    tokens_ref, w_x_ref, w_z_ref, w_xproj_ref, w_dt_ref, a_log_ref, w_out_ref, out_grad_ref,
    tok_s, og_s, end_s, sum_s, term_ref, rates_ref, own_ref, other_ref, sems, out_sems,
):
    leaving = []

    def leave(src, dst):
        copy = pltpu.make_async_copy(src, dst, out_sems.at[len(leaving)])
        copy.start()
        leaving.append(copy)

    copies = fetch(
        (
            (tokens_hbm, tokens_ref),
            (w_in_hbm.at[:, 0:C], w_x_ref),
            (w_xproj_hbm, w_xproj_ref),
            (w_dt_hbm, w_dt_ref),
            (a_log_hbm, a_log_ref),
            (w_in_hbm.at[:, C : 2 * C], w_z_ref),
            (out_grad_hbm, out_grad_ref),
            (w_out_hbm, w_out_ref),
        ),
        sems,
        5,
    )
    tok_s[...] = jnp.zeros_like(tok_s)
    og_s[...] = jnp.zeros_like(og_s)
    copies[0].wait()
    for i in range(T):
        tok_s[i, 0:T, :] = tokens_ref[i]
    tok = tok_s[...].reshape(CELLS, C)
    copies[1].wait()
    for copy in copies[5:]:
        copy.start()
    x_pre = jnp.dot(tok, w_x_ref[...], preferred_element_type=F32)
    x_pre_ref[...] = x_pre
    x_act = (x_pre * jax.nn.sigmoid(x_pre)).astype(BF16)
    copies[2].wait()
    leave(x_pre_ref, x_pre_hbm)
    dt_low = nt(x_act, w_xproj_ref[...])[:, 0:48].astype(BF16)
    x_dbl_t = nt(w_xproj_ref[...], x_act)
    for i in range(T):
        for j in range(T):
            cell = PAD * i + j
            b_ref[cell] = jnp.broadcast_to(x_dbl_t[48:64, cell : cell + 1], (N, 128))
            c_ref[cell] = jnp.broadcast_to(x_dbl_t[64:80, cell : cell + 1], (N, 128))
    leave(b_ref, b_hbm)
    leave(c_ref, c_hbm)
    copies[3].wait()
    dt_pre = jnp.dot(dt_low, w_dt_ref[...], preferred_element_type=F32) + dt_bias_ref[...]
    dt_pre_ref[...] = dt_pre
    step = jnp.maximum(dt_pre, 0.0) + jnp.log1p(jnp.exp(-jnp.abs(dt_pre)))
    step_ref[...] = step.reshape(T, PAD, C)
    x_full = x_act.astype(F32)
    x_ref[...] = x_full
    u_ref[...] = (step * x_full).reshape(T, PAD, C)
    leave(dt_pre_ref, dt_pre_hbm)
    leave(step_ref, step_hbm)
    leave(x_ref, x_hbm)
    leave(u_ref, u_hbm)
    copies[4].wait()
    rates_ref[...] = -jnp.exp(a_log_ref[...]) * LOG2E
    leave(rates_ref, rates_hbm)
    copies[5].wait()
    z_pre = jnp.dot(tok, w_z_ref[...], preferred_element_type=F32)
    z_pre_ref[...] = z_pre
    leave(z_pre_ref, z_pre_hbm)
    copies[6].wait()
    for i in range(T):
        og_s[i, 0:T, :] = out_grad_ref[i]
    copies[7].wait()
    gated = nt(og_s[...].reshape(CELLS, C), w_out_ref[...])
    gated_ref[...] = gated
    grad_ref[...] = (gated * (z_pre * jax.nn.sigmoid(z_pre))).reshape(T, PAD, C)
    leave(gated_ref, gated_hbm)
    leave(grad_ref, grad_hbm)
    term_ref[...] = jnp.zeros_like(term_ref)

    def one_row(back, carry):
        i = T - 1 - back
        row = [jnp.zeros((N, 128), F32) for _ in LANES]
        for j in range(T):
            b = b_ref[PAD * i + j]
            c = c_ref[PAD * i + j]
            for k, lanes in enumerate(LANES):
                decay = jnp.exp2(rates_ref[:, lanes] * step_ref[i, j : j + 1, lanes])
                row[k] = decay * row[k] + b * u_ref[i, j : j + 1, lanes]
                term_ref[j, :, lanes] = decay * (
                    c * grad_ref[i, j : j + 1, lanes] + term_ref[j, :, lanes]
                )
        for k, lanes in enumerate(LANES):
            end_s[i, :, lanes] = row[k]
        return carry

    lax.fori_loop(0, T, one_row, 0)
    leave(term_ref, term_hbm)
    for i in range(T):
        sum_s[i : i + 1, :] = jnp.sum(step_ref[i, 0:T, :], axis=0, keepdims=True)
    core = lax.axis_index("col") % 2
    for ref, out, half in ((other_ref, other_hbm, 1 - core), (own_ref, own_hbm, core)):
        pack_half(one_half(ref), 0, end_s, half)
        pack_sums(one_half(ref), 72, sum_s, half)
        leave(ref, out)
    for copy in leaving:
        copy.wait()


def chip_decay(core, rates_ref, part, group, t, k):
    states = 8 * ((3 * group + t) % 2)
    u = (3 * group + t) // 2 - 3 * group // 2
    rate = rates_ref[states : states + 8, half_lanes(core, k)]
    return jnp.exp2(rate * part[72 + 3 * u + k : 73 + 3 * u + k, :])


def combine_kernel(reverse, own_ref, got_ref, own_sums_ref, got_sums_ref, rates_ref, out_ref):
    core = lax.axis_index("col") % 2
    own_first = core == (1 if reverse else 0)
    for group in range(8):
        own, got = own_ref[group], got_ref[group]
        own_sums, got_sums = own_sums_ref[group], got_sums_ref[group]
        early, late = jnp.where(own_first, own, got), jnp.where(own_first, got, own)
        late_sums = jnp.where(own_first, got_sums, own_sums)
        for t in range(3):
            for k in range(3):
                rows = slice(8 * (3 * t + k), 8 * (3 * t + k) + 8)
                decay = chip_decay(core, rates_ref, late_sums, group, t, k)
                out_ref[group, rows, :] = decay * early[rows] + late[rows]
        if not reverse:
            out_ref[group, 72:80, :] = own[72:80] + got[72:80]


def split_kernel(
    reverse, state_ref, own_ref, got_ref, own_sums_ref, got_sums_ref, rates_ref, keep_ref, send_ref
):
    core = lax.axis_index("col") % 2
    own_first = core == (1 if reverse else 0)
    for group in range(8):
        early = jnp.where(own_first, own_ref[group], got_ref[group])
        early_sums = jnp.where(own_first, own_sums_ref[group], got_sums_ref[group])
        for t in range(3):
            for k in range(3):
                rows = slice(8 * (3 * t + k), 8 * (3 * t + k) + 8)
                state = state_ref[group, rows, :]
                through = (
                    chip_decay(core, rates_ref, early_sums, group, t, k) * state + early[rows]
                )
                keep_ref[group, rows, :] = jnp.where(own_first, state, through)
                send_ref[group, rows, :] = jnp.where(own_first, through, state)


def stage_kernel(own_ref, rates_ref, own_out, rates_out):
    own_out[...] = own_ref[...]
    rates_out[...] = rates_ref[...]


def prefix_kernel(axis, spans, sum_base, got_ref, sums_ref, rates_ref, out_ref):
    me = lax.axis_index(axis)
    group, half = me // 2, me % 2
    tiles = got_ref.shape[0]
    for t in range(3):
        states = pl.multiple_of(8 * ((3 * group + t) % 2), 8)
        later = (3 * group + t) // 2 > (3 * group) // 2
        for k in range(3):
            rate = rates_ref[pl.ds(states, 8), half_lanes(half, k)]
            for base, reverse in spans:
                state = jnp.zeros((8, 128), F32)
                rows = slice(base + 8 * (3 * t + k), base + 8 * (3 * t + k) + 8)
                for hop in range(tiles):
                    tile = tiles - 1 - hop if reverse else hop
                    out_ref[tile, rows, :] = state
                    total = jnp.where(
                        later,
                        sums_ref[tile, sum_base + 3 + k : sum_base + 4 + k, :],
                        sums_ref[tile, sum_base + k : sum_base + k + 1, :],
                    )
                    state = jnp.exp2(rate * total) * state + got_ref[tile, rows, :]


def forward_kernel(
    keep_ref, came_ref, rates_s, step_ref, u_ref, b_ref, term_ref, sent_ref, row_s, col_s, sum_s
):
    core = lax.axis_index("col") % 2
    unpack_half(row_s, one_half(keep_ref), 0, core)
    unpack_half(row_s, one_half(came_ref), 0, 1 - core)
    col_s[...] = jnp.zeros_like(col_s)

    def one_row(i, carry):
        row = [row_s[i, :, lanes] for lanes in LANES]
        for j in range(T):
            b = b_ref[PAD * i + j]
            for k, lanes in enumerate(LANES):
                decay = jnp.exp2(rates_s[:, lanes] * step_ref[i, j : j + 1, lanes])
                row[k] = decay * row[k] + b * u_ref[i, j : j + 1, lanes]
                col_s[j, :, lanes] = decay * col_s[j, :, lanes] + row[k]
        return carry

    lax.fori_loop(0, T, one_row, 0)
    total = step_ref[0]
    for i in range(1, T):
        total = total + step_ref[i]
    sum_s[...] = total
    for half, chunk_of in enumerate(both_halves(sent_ref)):
        pack_half(chunk_of, 0, col_s, half)
        pack_half(chunk_of, 72, term_ref, half)
        pack_sums(chunk_of, 144, sum_s, half)


def backward_kernel(
    col_got_ref, rates_s, step_ref, grad_ref, c_ref, own_ref, other_ref, term_s, end_s
):
    for half, chunk_of in enumerate(both_halves(col_got_ref)):
        unpack_half(term_s, chunk_of, 72, half)

    def one_row(back, carry):
        i = T - 1 - back
        row = [jnp.zeros((N, 128), F32) for _ in LANES]
        for j in reversed(range(T)):
            c = c_ref[PAD * i + j]
            for k, lanes in enumerate(LANES):
                decay = jnp.exp2(rates_s[:, lanes] * step_ref[i, j : j + 1, lanes])
                adjoint = c * grad_ref[i, j : j + 1, lanes] + term_s[j, :, lanes]
                term_s[j, :, lanes] = decay * adjoint
                row[k] = decay * (adjoint + row[k])
        for k, lanes in enumerate(LANES):
            end_s[i, :, lanes] = row[k]
        return carry

    lax.fori_loop(0, T, one_row, 0)
    core = lax.axis_index("col") % 2
    pack_half(one_half(own_ref), 0, end_s, core)
    pack_half(one_half(other_ref), 0, end_s, 1 - core)


def put_part(part_ref, i, j, k, values):
    rows = pl.ds(pl.multiple_of(8 * (PAD * i + j), 8), 8)
    part_ref[k, rows, :] = values[0:8] + values[8:16]


def add_parts(sum_ref, part_ref, i, turns=range(T)):
    for turn in turns:
        j, k = 8 * (turn // 6), turn % 6
        base = 8 * (PAD * i + j)
        total = part_ref[k, pl.ds(base, 8, stride=8), :]
        for r in range(1, 8):
            total = total + part_ref[k, pl.ds(base + r, 8, stride=8), :]
        sum_ref[i, j : j + 8, LANES[k]] = total


def last_kernel(
    keep_ref, came_ref, col_got_ref, back_keep_ref, back_came_ref, x_pre_ref, z_pre_ref, dt_pre_ref, gated_ref, step_ref,
    u_ref, x_ref, grad_ref, b_ref, c_ref, rates_s, d_skip_ref, w_in_hbm, w_xproj_hbm, w_dt_hbm,
    w_out_hbm,
    layer_hbm, token_hbm,
    w_in_ref, w_xproj_ref, w_dt_ref, w_out_ref, layer_ref, token_ref,
    row_s, col_s, full_keep, row_keep, scan_s, step_sum_s, x_sum_s, b_part, c_part, part_a, part_b, w_dt_s, act_s,
    z_part_s, dbl_s, sems,
):
    copies = fetch(
        (
            (w_out_hbm, w_out_ref),
            (w_dt_hbm, w_dt_ref),
            (w_xproj_hbm, w_xproj_ref),
            (w_in_hbm, w_in_ref),
        ),
        sems,
    )
    core = lax.axis_index("col") % 2
    unpack_half(row_s, one_half(keep_ref), 0, core)
    unpack_half(row_s, one_half(came_ref), 0, 1 - core)
    for half, chunk_of in enumerate(both_halves(col_got_ref)):
        unpack_half(col_s, chunk_of, 0, half)
    for ref in (b_part, c_part):
        ref[...] = jnp.zeros_like(ref)

    def down_row(i, carry):
        before = jnp.maximum(i - 1, 0)
        row = [row_s[i, :, lanes] for lanes in LANES]
        for j in range(T):
            cell = PAD * i + j
            b = b_ref[cell]
            c = c_ref[cell]
            part = jnp.zeros((N, 128), F32)
            for k, lanes in enumerate(LANES):
                decay = jnp.exp2(rates_s[:, lanes] * step_ref[i, j : j + 1, lanes])
                row_old = decay * row[k]
                row[k] = row_old + b * u_ref[i, j : j + 1, lanes]
                full_old = decay * col_s[j, :, lanes]
                full = full_old + row[k]
                col_s[j, :, lanes] = full
                row_keep[T * i + j, :, lanes] = row_old
                full_keep[T * i + j, :, lanes] = full_old
                put_part(part_a, i, j, k, c * full)
                part = part + full * grad_ref[i, j : j + 1, lanes]
            c_part[cell] = part
            add_parts(scan_s, part_a, before, (j,))
        return carry

    lax.fori_loop(0, T, down_row, 0)
    add_parts(scan_s, part_a, T - 1)
    skip = d_skip_ref[...]
    for i in range(T):
        rows = slice(PAD * i, PAD * i + PAD)
        z_pre = z_pre_ref[rows, :]
        scan_out = scan_s[i] + skip * x_ref[rows, :]
        z_sig = jax.nn.sigmoid(z_pre)
        act_s[rows, :] = (scan_out * (z_pre * z_sig)).astype(BF16)
        z_part_s[rows, :] = (
            gated_ref[rows, :] * scan_out * (z_sig * (1.0 + z_pre * (1.0 - z_sig)))
        ).astype(BF16)
    copies[0].wait()
    layer = jnp.dot(act_s[...], w_out_ref[...], preferred_element_type=F32).astype(BF16)
    for i in range(T):
        layer_ref[i] = layer[PAD * i : PAD * i + T, :]
    layer_copy = pltpu.make_async_copy(layer_ref, layer_hbm, sems.at[4])
    layer_copy.start()
    for half, chunk_of in enumerate(both_halves(col_got_ref)):
        unpack_half(col_s, chunk_of, 72, half)
    unpack_half(row_s, one_half(back_keep_ref), 0, core)
    unpack_half(row_s, one_half(back_came_ref), 0, 1 - core)

    def up_row(back, carry):
        i = T - 1 - back
        before = jnp.minimum(i + 1, T - 1)
        row = [row_s[i, :, lanes] for lanes in LANES]
        for j in reversed(range(T)):
            cell = PAD * i + j
            b = b_ref[cell]
            c = c_ref[cell]
            part = jnp.zeros((N, 128), F32)
            for k, lanes in enumerate(LANES):
                decay = jnp.exp2(rates_s[:, lanes] * step_ref[i, j : j + 1, lanes])
                col_adjoint = c * grad_ref[i, j : j + 1, lanes] + col_s[j, :, lanes]
                col_s[j, :, lanes] = decay * col_adjoint
                row_adjoint = col_adjoint + row[k]
                row[k] = decay * row_adjoint
                decay_grad = (
                    col_adjoint * full_keep[T * i + j, :, lanes] + row_adjoint * row_keep[T * i + j, :, lanes]
                )
                put_part(part_a, i, j, k, decay_grad * rates_s[:, lanes])
                put_part(part_b, i, j, k, row_adjoint * b)
                part = part + row_adjoint * u_ref[i, j : j + 1, lanes]
            b_part[cell] = part
            add_parts(step_sum_s, part_a, before, (j,))
            add_parts(x_sum_s, part_b, before, (j,))
        return carry

    lax.fori_loop(0, T, up_row, 0)
    add_parts(step_sum_s, part_a, 0)
    add_parts(x_sum_s, part_b, 0)

    state = lax.broadcasted_iota(jnp.int32, (PAD * N, 80), 0) % N
    col = lax.broadcasted_iota(jnp.int32, (PAD * N, 80), 1)
    at_b, at_c = col == state + 48, col == state + 64
    cell = lax.broadcasted_iota(jnp.int32, (PAD, PAD * N), 0)
    choose = lax.broadcasted_iota(jnp.int32, (PAD, PAD * N), 1) // N == cell
    choose = choose.astype(F32).astype(BF16)
    for i in range(T):
        rows = slice(PAD * i, PAD * i + PAD)
        step_grad = step_sum_s[i] * (1.0 / LOG2E) + x_sum_s[i] * x_ref[rows, :]
        act_s[rows, :] = (step_grad * jax.nn.sigmoid(dt_pre_ref[rows, :])).astype(BF16)
        b_sum = jnp.sum(b_part[rows].reshape(PAD * N, 128), axis=1, keepdims=True)
        c_sum = jnp.sum(c_part[rows].reshape(PAD * N, 128), axis=1, keepdims=True)
        placed = jnp.where(at_b, b_sum, jnp.where(at_c, c_sum, 0.0)).astype(BF16)
        dbl_s[rows, :] = jnp.dot(choose, placed, preferred_element_type=F32)
    copies[1].wait()
    w_dt_s[...] = jnp.zeros_like(w_dt_s)
    w_dt_s[0:48, :] = w_dt_ref[...]
    dbl = (nt(act_s[...], w_dt_s[...]) + dbl_s[...]).astype(BF16)
    copies[2].wait()
    step_sum_s[...] = jnp.dot(dbl, w_xproj_ref[...], preferred_element_type=F32).reshape(T, PAD, C)
    for i in range(T):
        rows = slice(PAD * i, PAD * i + PAD)
        x_pre = x_pre_ref[rows, :]
        x_grad = x_sum_s[i] * step_ref[i] + grad_ref[i] * skip + step_sum_s[i]
        x_sig = jax.nn.sigmoid(x_pre)
        act_s[rows, :] = (x_grad * (x_sig * (1.0 + x_pre * (1.0 - x_sig)))).astype(BF16)
    copies[3].wait()
    token = (nt(act_s[...], w_in_ref[:, 0:C]) + nt(z_part_s[...], w_in_ref[:, C : 2 * C])).astype(
        BF16
    )
    for i in range(T):
        token_ref[i] = token[PAD * i : PAD * i + T, :]
    token_copy = pltpu.make_async_copy(token_ref, token_hbm, sems.at[5])
    token_copy.start()
    layer_copy.wait()
    token_copy.wait()


IN_VMEM = pl.BlockSpec(memory_space=pltpu.VMEM)
IN_HBM = pl.BlockSpec(memory_space=pltpu.HBM)


def call(kernel, out_shape, scratch, name, limit, *args, fetched=(), sent=()):
    many = isinstance(out_shape, tuple)
    return pl.pallas_call(
        kernel,
        out_shape=out_shape,
        in_specs=[IN_HBM if k in fetched else IN_VMEM for k in range(len(args))],
        out_specs=tuple(IN_HBM if k in sent else IN_VMEM for k in range(len(out_shape)))
        if many
        else IN_VMEM,
        scratch_shapes=scratch,
        name=name,
        compiler_params=pltpu.CompilerParams(vmem_limit_bytes=limit * 1024 * 1024),
    )(*args)


def f32(*shape):
    return jax.ShapeDtypeStruct(shape, F32)


def vmem(*shape):
    return pltpu.VMEM(shape, F32)


def prefix(axis, spans, sum_base, rows, got, sums, rates):
    def kernel(got_ref, sums_ref, rates_ref, out_ref):
        prefix_kernel(axis, spans, sum_base, got_ref, sums_ref, rates_ref, out_ref)

    out = f32(got.shape[0], rows, 128)
    return call(kernel, out, (), "prefix_" + axis, 4, got, sums, rates)


def swap(sent, axis, groups=None):
    return lax.all_to_all(sent, axis, 0, 0, tiled=True, axis_index_groups=groups)


def row_scan(own, got, sums, rates, reverse):
    partner = [(place, place ^ 1) for place in range(16)]
    same_core = [[2 * chip + core for chip in range(8)] for core in range(2)]
    if sums is None:
        sums = (own, got)

    def combine(*refs):
        combine_kernel(reverse, *refs)

    def split(*refs):
        split_kernel(reverse, *refs)

    chip = call(
        combine, f32(8, own.shape[1], 128), (), "combine", 6, own, got, *sums[:2], rates
    )
    chips = swap(chip, "col", same_core)
    chip_sums = chips if len(sums) == 2 else sums[2]
    state = swap(
        prefix("col", ((0, reverse),), 72, 72, chips, chip_sums, rates), "col", same_core
    )
    half = f32(8, 72, 128)
    keep, send = call(split, (half, half), (), "split", 6, state, own, got, *sums[:2], rates)
    return keep, lax.ppermute(send, "col", partner), (*sums[:2], chip_sums)


def body(tokens, w_in, w_xproj, w_dt, dt_bias, a_log, d_skip, w_out, out_grad):
    edge, wide, dense = vmem(T, N, C), vmem(T, PAD, C), vmem(CELLS, C)
    flat, grid, spread = f32(CELLS, C), f32(T, PAD, C), f32(CELLS, N, 128)
    kept, sums, parts = vmem(T * T, N, C), vmem(PAD, C), vmem(C // 128, 8 * CELLS, 128)
    padded, cells = pltpu.VMEM((T, PAD, C), BF16), pltpu.VMEM((T, T, C), BF16)
    square, narrow = pltpu.VMEM((C, C), BF16), pltpu.VMEM((80, C), BF16)
    halves = vmem(8, 80, 128)
    low_rank, half_width = pltpu.VMEM((48, C), BF16), pltpu.VMEM((CELLS, C), BF16)
    w_xproj = w_xproj.T
    partner = [(place, place ^ 1) for place in range(16)]
    x_pre, z_pre, dt_pre, gated, step, u, x, grad, b, c, term, rates, own, other = call(
        first_kernel,
        (
            flat, flat, flat, flat, grid, grid, flat, grid, spread, spread, f32(T, N, C),
            f32(N, C), f32(8, 80, 128), f32(8, 80, 128),
        ),
        (
            dense, dense, dense, dense, wide, wide, dense, wide, vmem(CELLS, N, 128),
            vmem(CELLS, N, 128), cells, square, square, narrow, low_rank, vmem(N, C), square, cells,
            padded, padded, edge, sums, edge, vmem(N, C), halves, halves,
            pltpu.SemaphoreType.DMA((8,)), pltpu.SemaphoreType.DMA((14,)),
        ),
        "first", 54,
        tokens, w_in, w_xproj, w_dt, a_log, w_out, out_grad, dt_bias,
        fetched=range(7), sent=range(14),
    )
    got = lax.ppermute(other, "col", partner)
    own, rates = call(
        stage_kernel, (f32(8, 80, 128), f32(N, C)), (), "stage", 4, own, rates
    )
    keep, came, chip_sums = row_scan(own, got, None, rates, False)
    col_sent = call(
        forward_kernel, f32(16, 152, 128), (edge, edge, sums), "forward", 6,
        keep, came, rates, step, u, b, term,
    )
    col_all = swap(col_sent, "row")
    col_got = swap(
        prefix("row", ((0, False), (72, True)), 144, 144, col_all, col_all, rates), "row"
    )
    back_half = f32(8, 72, 128)
    back_own, back_other = call(
        backward_kernel, (back_half, back_half), (edge, edge), "backward", 6,
        col_got, rates, step, grad, c,
    )
    back_got = lax.ppermute(back_other, "col", partner)
    back_keep, back_came, chip_sums = row_scan(back_own, back_got, chip_sums, rates, True)
    out = jax.ShapeDtypeStruct((T, T, C), BF16)
    return call(
        last_kernel,
        (out, out),
        (
            pltpu.VMEM((C, 2 * C), BF16), narrow, low_rank, square, cells, cells,
            edge, edge, kept, kept, wide, wide, wide, vmem(CELLS, N, 128),
            vmem(CELLS, N, 128), parts, parts, narrow, half_width, half_width, vmem(CELLS, 80),
            pltpu.SemaphoreType.DMA((6,)),
        ),
        "last", 42,
        keep, came, col_got, back_keep, back_came, x_pre, z_pre, dt_pre, gated, step, u, x, grad, b, c, rates,
        d_skip, w_in, w_xproj, w_dt, w_out,
        fetched=range(17, 21), sent=range(2),
    )


def solution(mesh):
    return jax.shard_map(
        body,
        mesh=mesh,
        in_specs=(P("row", "col", None), P(), P(), P(), P(), P(), P(), P(), P("row", "col", None)),
        out_specs=(P("row", "col", None), P("row", "col", None)),
        check_vma=False,
    )
```

```python
import jax
import jax.numpy as jnp
from jax import lax
from jax.experimental import pallas as pl
from jax.experimental.pallas import tpu as pltpu
from jax.sharding import PartitionSpec as P

LOG2E = 1.4426950408889634
T = 12
PAD = 16
CELLS = T * PAD
N = 16
C = 768
HALF = 384
LANES = [slice(128 * k, 128 * k + 128) for k in range(C // 128)]
F32, BF16 = jnp.float32, jnp.bfloat16


def nt(left, right):
    return lax.dot_general(left, right, (((1,), (1,)), ((), ())), preferred_element_type=F32)


def pieces():
    for i in range(T):
        for h in range(2):
            q = 2 * i + h
            for k in range(3):
                yield i, slice(8 * h, 8 * h + 8), k, q // 3, 8 * (3 * (q % 3) + k)


def half_lanes(half, k):
    if isinstance(half, int):
        return slice(HALF * half + 128 * k, HALF * half + 128 * k + 128)
    return pl.ds(pl.multiple_of(HALF * half + 128 * k, 128), 128)


def pack_half(chunk_of, base, edge_ref, half):
    for i, states, k, group, row in pieces():
        chunk_of(group)[base + row : base + row + 8, :] = edge_ref[i, states, half_lanes(half, k)]


def unpack_half(edge_ref, chunk_of, base, half):
    for i, states, k, group, row in pieces():
        edge_ref[i, states, half_lanes(half, k)] = chunk_of(group)[base + row : base + row + 8, :]


def pack_sums(chunk_of, base, sum_ref, half):
    for group in range(8):
        rows = [
            sum_ref[pl.ds(3 * group // 2 + u, 1), half_lanes(half, k)]
            for u in range(2)
            for k in range(3)
        ]
        chunk_of(group)[base : base + 8, :] = jnp.concatenate(
            rows + [jnp.zeros((2, 128), F32)], axis=0
        )


def both_halves(ref):
    return [(lambda group, half=half: ref.at[2 * group + half]) for half in range(2)]


def one_half(ref):
    return lambda group: ref.at[group]


def fetch(pairs, sems, now=None):
    copies = [pltpu.make_async_copy(src, dst, sems.at[k]) for k, (src, dst) in enumerate(pairs)]
    for copy in copies[:now]:
        copy.start()
    return copies


def first_kernel(
    tokens_hbm, w_in_hbm, w_xproj_hbm, w_dt_hbm, a_log_hbm, dt_bias_ref,
    x_pre_hbm, dt_pre_hbm, step_hbm, u_hbm, x_hbm, b_hbm, c_hbm, rates_hbm, own_hbm, other_hbm,
    x_pre_ref, dt_pre_ref, step_ref, u_ref, x_ref, b_ref, c_ref,
    tokens_ref, w_x_ref, w_xproj_ref, w_dt_ref, a_log_ref,
    tok_s, end_s, sum_s, rates_ref, own_ref, other_ref, sems, out_sems,
):
    leaving = []

    def leave(src, dst):
        copy = pltpu.make_async_copy(src, dst, out_sems.at[len(leaving)])
        copy.start()
        leaving.append(copy)

    copies = fetch(
        (
            (tokens_hbm, tokens_ref),
            (w_in_hbm.at[:, 0:C], w_x_ref),
            (w_xproj_hbm, w_xproj_ref),
            (w_dt_hbm, w_dt_ref),
            (a_log_hbm, a_log_ref),
        ),
        sems,
    )
    tok_s[...] = jnp.zeros_like(tok_s)
    copies[0].wait()
    for i in range(T):
        tok_s[i, 0:T, :] = tokens_ref[i]
    tok = tok_s[...].reshape(CELLS, C)
    copies[1].wait()
    x_pre = jnp.dot(tok, w_x_ref[...], preferred_element_type=F32)
    x_pre_ref[...] = x_pre
    x_act = (x_pre * jax.nn.sigmoid(x_pre)).astype(BF16)
    copies[2].wait()
    leave(x_pre_ref, x_pre_hbm)
    dt_low = nt(x_act, w_xproj_ref[...])[:, 0:48].astype(BF16)
    x_dbl_t = nt(w_xproj_ref[...], x_act)
    for i in range(T):
        for j in range(T):
            cell = PAD * i + j
            b_ref[cell] = jnp.broadcast_to(x_dbl_t[48:64, cell : cell + 1], (N, 128))
            c_ref[cell] = jnp.broadcast_to(x_dbl_t[64:80, cell : cell + 1], (N, 128))
    leave(b_ref, b_hbm)
    leave(c_ref, c_hbm)
    copies[3].wait()
    dt_pre = jnp.dot(dt_low, w_dt_ref[...], preferred_element_type=F32) + dt_bias_ref[...]
    dt_pre_ref[...] = dt_pre
    step = jnp.maximum(dt_pre, 0.0) + jnp.log1p(jnp.exp(-jnp.abs(dt_pre)))
    step_ref[...] = step.reshape(T, PAD, C)
    x_full = x_act.astype(F32)
    x_ref[...] = x_full
    u_ref[...] = (step * x_full).reshape(T, PAD, C)
    leave(dt_pre_ref, dt_pre_hbm)
    leave(step_ref, step_hbm)
    leave(x_ref, x_hbm)
    leave(u_ref, u_hbm)
    copies[4].wait()
    rates_ref[...] = -jnp.exp(a_log_ref[...]) * LOG2E
    leave(rates_ref, rates_hbm)

    def one_row(back, carry):
        i = T - 1 - back
        row = [jnp.zeros((N, 128), F32) for _ in LANES]
        for j in range(T):
            b = b_ref[PAD * i + j]
            for k, lanes in enumerate(LANES):
                decay = jnp.exp2(rates_ref[:, lanes] * step_ref[i, j : j + 1, lanes])
                row[k] = decay * row[k] + b * u_ref[i, j : j + 1, lanes]
        for k, lanes in enumerate(LANES):
            end_s[i, :, lanes] = row[k]
        return carry

    lax.fori_loop(0, T, one_row, 0)
    for i in range(T):
        sum_s[i : i + 1, :] = jnp.sum(step_ref[i, 0:T, :], axis=0, keepdims=True)
    core = lax.axis_index("col") % 2
    for ref, out, half in ((other_ref, other_hbm, 1 - core), (own_ref, own_hbm, core)):
        pack_half(one_half(ref), 0, end_s, half)
        pack_sums(one_half(ref), 72, sum_s, half)
        leave(ref, out)
    for copy in leaving:
        copy.wait()


def gate_kernel(
    after_hbm, tokens_ref, out_grad_ref, w_in_ref, w_out_ref, step_ref, c_ref, rates_ref,
    z_pre_ref, gated_ref, grad_ref, term_ref, rates_out,
    tok_s, og_s,
):
    tok_s[...] = jnp.zeros_like(tok_s)
    og_s[...] = jnp.zeros_like(og_s)
    for i in range(T):
        tok_s[i, 0:T, :] = tokens_ref[i]
        og_s[i, 0:T, :] = out_grad_ref[i]
    tok = tok_s[...].reshape(CELLS, C)
    z_pre = jnp.dot(tok, w_in_ref[:, C : 2 * C], preferred_element_type=F32)
    z_pre_ref[...] = z_pre
    gated = nt(og_s[...].reshape(CELLS, C), w_out_ref[...])
    gated_ref[...] = gated
    grad_ref[...] = (gated * (z_pre * jax.nn.sigmoid(z_pre))).reshape(T, PAD, C)
    term_ref[...] = jnp.zeros_like(term_ref)
    rates_out[...] = rates_ref[...]

    def one_row(back, carry):
        i = T - 1 - back
        for j in range(T):
            c = c_ref[PAD * i + j]
            for lanes in LANES:
                decay = jnp.exp2(rates_ref[:, lanes] * step_ref[i, j : j + 1, lanes])
                term_ref[j, :, lanes] = decay * (
                    c * grad_ref[i, j : j + 1, lanes] + term_ref[j, :, lanes]
                )
        return carry

    lax.fori_loop(0, T, one_row, 0)


def chip_decay(core, rates_ref, part, group, t, k):
    states = 8 * ((3 * group + t) % 2)
    u = (3 * group + t) // 2 - 3 * group // 2
    rate = rates_ref[states : states + 8, half_lanes(core, k)]
    return jnp.exp2(rate * part[72 + 3 * u + k : 73 + 3 * u + k, :])


def combine_kernel(reverse, own_ref, got_ref, own_sums_ref, got_sums_ref, rates_ref, out_ref):
    core = lax.axis_index("col") % 2
    own_first = core == (1 if reverse else 0)
    for group in range(8):
        own, got = own_ref[group], got_ref[group]
        own_sums, got_sums = own_sums_ref[group], got_sums_ref[group]
        early, late = jnp.where(own_first, own, got), jnp.where(own_first, got, own)
        late_sums = jnp.where(own_first, got_sums, own_sums)
        for t in range(3):
            for k in range(3):
                rows = slice(8 * (3 * t + k), 8 * (3 * t + k) + 8)
                decay = chip_decay(core, rates_ref, late_sums, group, t, k)
                out_ref[group, rows, :] = decay * early[rows] + late[rows]
        if not reverse:
            out_ref[group, 72:80, :] = own[72:80] + got[72:80]


def split_kernel(
    reverse, state_ref, own_ref, got_ref, own_sums_ref, got_sums_ref, rates_ref, keep_ref, send_ref
):
    core = lax.axis_index("col") % 2
    own_first = core == (1 if reverse else 0)
    for group in range(8):
        early = jnp.where(own_first, own_ref[group], got_ref[group])
        early_sums = jnp.where(own_first, own_sums_ref[group], got_sums_ref[group])
        for t in range(3):
            for k in range(3):
                rows = slice(8 * (3 * t + k), 8 * (3 * t + k) + 8)
                state = state_ref[group, rows, :]
                through = (
                    chip_decay(core, rates_ref, early_sums, group, t, k) * state + early[rows]
                )
                keep_ref[group, rows, :] = jnp.where(own_first, state, through)
                send_ref[group, rows, :] = jnp.where(own_first, through, state)


def stage_kernel(own_ref, rates_ref, own_out, rates_out):
    own_out[...] = own_ref[...]
    rates_out[...] = rates_ref[...]


def prefix_kernel(axis, spans, sum_base, got_ref, sums_ref, rates_ref, out_ref):
    me = lax.axis_index(axis)
    group, half = me // 2, me % 2
    tiles = got_ref.shape[0]
    for t in range(3):
        states = pl.multiple_of(8 * ((3 * group + t) % 2), 8)
        later = (3 * group + t) // 2 > (3 * group) // 2
        for k in range(3):
            rate = rates_ref[pl.ds(states, 8), half_lanes(half, k)]
            for base, reverse in spans:
                state = jnp.zeros((8, 128), F32)
                rows = slice(base + 8 * (3 * t + k), base + 8 * (3 * t + k) + 8)
                for hop in range(tiles):
                    tile = tiles - 1 - hop if reverse else hop
                    out_ref[tile, rows, :] = state
                    total = jnp.where(
                        later,
                        sums_ref[tile, sum_base + 3 + k : sum_base + 4 + k, :],
                        sums_ref[tile, sum_base + k : sum_base + k + 1, :],
                    )
                    state = jnp.exp2(rate * total) * state + got_ref[tile, rows, :]


def forward_kernel(
    keep_ref, came_ref, rates_s, step_ref, u_ref, b_ref, term_ref, sent_ref, row_s, col_s, sum_s
):
    core = lax.axis_index("col") % 2
    unpack_half(row_s, one_half(keep_ref), 0, core)
    unpack_half(row_s, one_half(came_ref), 0, 1 - core)
    col_s[...] = jnp.zeros_like(col_s)

    def one_row(i, carry):
        row = [row_s[i, :, lanes] for lanes in LANES]
        for j in range(T):
            b = b_ref[PAD * i + j]
            for k, lanes in enumerate(LANES):
                decay = jnp.exp2(rates_s[:, lanes] * step_ref[i, j : j + 1, lanes])
                row[k] = decay * row[k] + b * u_ref[i, j : j + 1, lanes]
                col_s[j, :, lanes] = decay * col_s[j, :, lanes] + row[k]
        return carry

    lax.fori_loop(0, T, one_row, 0)
    total = step_ref[0]
    for i in range(1, T):
        total = total + step_ref[i]
    sum_s[...] = total
    for half, chunk_of in enumerate(both_halves(sent_ref)):
        pack_half(chunk_of, 0, col_s, half)
        pack_half(chunk_of, 72, term_ref, half)
        pack_sums(chunk_of, 144, sum_s, half)


def backward_kernel(
    col_got_ref, rates_s, step_ref, grad_ref, c_ref, own_ref, other_ref, term_s, end_s
):
    for half, chunk_of in enumerate(both_halves(col_got_ref)):
        unpack_half(term_s, chunk_of, 72, half)

    def one_row(back, carry):
        i = T - 1 - back
        row = [jnp.zeros((N, 128), F32) for _ in LANES]
        for j in reversed(range(T)):
            c = c_ref[PAD * i + j]
            for k, lanes in enumerate(LANES):
                decay = jnp.exp2(rates_s[:, lanes] * step_ref[i, j : j + 1, lanes])
                adjoint = c * grad_ref[i, j : j + 1, lanes] + term_s[j, :, lanes]
                term_s[j, :, lanes] = decay * adjoint
                row[k] = decay * (adjoint + row[k])
        for k, lanes in enumerate(LANES):
            end_s[i, :, lanes] = row[k]
        return carry

    lax.fori_loop(0, T, one_row, 0)
    core = lax.axis_index("col") % 2
    pack_half(one_half(own_ref), 0, end_s, core)
    pack_half(one_half(other_ref), 0, end_s, 1 - core)


def put_part(part_ref, i, j, k, values):
    rows = pl.ds(pl.multiple_of(8 * (PAD * i + j), 8), 8)
    part_ref[k, rows, :] = values[0:8] + values[8:16]


def add_parts(sum_ref, part_ref, i, turns=range(T)):
    for turn in turns:
        j, k = 8 * (turn // 6), turn % 6
        base = 8 * (PAD * i + j)
        total = part_ref[k, pl.ds(base, 8, stride=8), :]
        for r in range(1, 8):
            total = total + part_ref[k, pl.ds(base + r, 8, stride=8), :]
        sum_ref[i, j : j + 8, LANES[k]] = total


def last_kernel(
    keep_ref, came_ref, col_got_ref, back_keep_ref, back_came_ref, x_pre_ref, z_pre_ref, dt_pre_ref, gated_ref, step_ref,
    u_ref, x_ref, grad_ref, b_ref, c_ref, rates_s, d_skip_ref, w_in_hbm, w_xproj_hbm, w_dt_hbm,
    w_out_hbm,
    layer_hbm, token_hbm,
    w_in_ref, w_xproj_ref, w_dt_ref, w_out_ref, layer_ref, token_ref,
    row_s, col_s, full_keep, row_keep, scan_s, step_sum_s, x_sum_s, b_part, c_part, part_a, part_b, w_dt_s, act_s,
    z_part_s, dbl_s, sems,
):
    copies = fetch(
        (
            (w_out_hbm, w_out_ref),
            (w_dt_hbm, w_dt_ref),
            (w_xproj_hbm, w_xproj_ref),
            (w_in_hbm, w_in_ref),
        ),
        sems,
    )
    core = lax.axis_index("col") % 2
    unpack_half(row_s, one_half(keep_ref), 0, core)
    unpack_half(row_s, one_half(came_ref), 0, 1 - core)
    for half, chunk_of in enumerate(both_halves(col_got_ref)):
        unpack_half(col_s, chunk_of, 0, half)
    for ref in (b_part, c_part):
        ref[...] = jnp.zeros_like(ref)

    def down_row(i, carry):
        before = jnp.maximum(i - 1, 0)
        row = [row_s[i, :, lanes] for lanes in LANES]
        for j in range(T):
            cell = PAD * i + j
            b = b_ref[cell]
            c = c_ref[cell]
            part = jnp.zeros((N, 128), F32)
            for k, lanes in enumerate(LANES):
                decay = jnp.exp2(rates_s[:, lanes] * step_ref[i, j : j + 1, lanes])
                row_old = decay * row[k]
                row[k] = row_old + b * u_ref[i, j : j + 1, lanes]
                full_old = decay * col_s[j, :, lanes]
                full = full_old + row[k]
                col_s[j, :, lanes] = full
                row_keep[T * i + j, :, lanes] = row_old
                full_keep[T * i + j, :, lanes] = full_old
                put_part(part_a, i, j, k, c * full)
                part = part + full * grad_ref[i, j : j + 1, lanes]
            c_part[cell] = part
            add_parts(scan_s, part_a, before, (j,))
        return carry

    lax.fori_loop(0, T, down_row, 0)
    add_parts(scan_s, part_a, T - 1)
    skip = d_skip_ref[...]
    for i in range(T):
        rows = slice(PAD * i, PAD * i + PAD)
        z_pre = z_pre_ref[rows, :]
        scan_out = scan_s[i] + skip * x_ref[rows, :]
        z_sig = jax.nn.sigmoid(z_pre)
        act_s[rows, :] = (scan_out * (z_pre * z_sig)).astype(BF16)
        z_part_s[rows, :] = (
            gated_ref[rows, :] * scan_out * (z_sig * (1.0 + z_pre * (1.0 - z_sig)))
        ).astype(BF16)
    copies[0].wait()
    layer = jnp.dot(act_s[...], w_out_ref[...], preferred_element_type=F32).astype(BF16)
    for i in range(T):
        layer_ref[i] = layer[PAD * i : PAD * i + T, :]
    layer_copy = pltpu.make_async_copy(layer_ref, layer_hbm, sems.at[4])
    layer_copy.start()
    for half, chunk_of in enumerate(both_halves(col_got_ref)):
        unpack_half(col_s, chunk_of, 72, half)
    unpack_half(row_s, one_half(back_keep_ref), 0, core)
    unpack_half(row_s, one_half(back_came_ref), 0, 1 - core)

    def up_row(back, carry):
        i = T - 1 - back
        before = jnp.minimum(i + 1, T - 1)
        row = [row_s[i, :, lanes] for lanes in LANES]
        for j in reversed(range(T)):
            cell = PAD * i + j
            b = b_ref[cell]
            c = c_ref[cell]
            part = jnp.zeros((N, 128), F32)
            for k, lanes in enumerate(LANES):
                decay = jnp.exp2(rates_s[:, lanes] * step_ref[i, j : j + 1, lanes])
                col_adjoint = c * grad_ref[i, j : j + 1, lanes] + col_s[j, :, lanes]
                col_s[j, :, lanes] = decay * col_adjoint
                row_adjoint = col_adjoint + row[k]
                row[k] = decay * row_adjoint
                decay_grad = (
                    col_adjoint * full_keep[T * i + j, :, lanes] + row_adjoint * row_keep[T * i + j, :, lanes]
                )
                put_part(part_a, i, j, k, decay_grad * rates_s[:, lanes])
                put_part(part_b, i, j, k, row_adjoint * b)
                part = part + row_adjoint * u_ref[i, j : j + 1, lanes]
            b_part[cell] = part
            add_parts(step_sum_s, part_a, before, (j,))
            add_parts(x_sum_s, part_b, before, (j,))
        return carry

    lax.fori_loop(0, T, up_row, 0)
    add_parts(step_sum_s, part_a, 0)
    add_parts(x_sum_s, part_b, 0)

    state = lax.broadcasted_iota(jnp.int32, (PAD * N, 80), 0) % N
    col = lax.broadcasted_iota(jnp.int32, (PAD * N, 80), 1)
    at_b, at_c = col == state + 48, col == state + 64
    cell = lax.broadcasted_iota(jnp.int32, (PAD, PAD * N), 0)
    choose = lax.broadcasted_iota(jnp.int32, (PAD, PAD * N), 1) // N == cell
    choose = choose.astype(F32).astype(BF16)
    for i in range(T):
        rows = slice(PAD * i, PAD * i + PAD)
        step_grad = step_sum_s[i] * (1.0 / LOG2E) + x_sum_s[i] * x_ref[rows, :]
        act_s[rows, :] = (step_grad * jax.nn.sigmoid(dt_pre_ref[rows, :])).astype(BF16)
        b_sum = jnp.sum(b_part[rows].reshape(PAD * N, 128), axis=1, keepdims=True)
        c_sum = jnp.sum(c_part[rows].reshape(PAD * N, 128), axis=1, keepdims=True)
        placed = jnp.where(at_b, b_sum, jnp.where(at_c, c_sum, 0.0)).astype(BF16)
        dbl_s[rows, :] = jnp.dot(choose, placed, preferred_element_type=F32)
    copies[1].wait()
    w_dt_s[...] = jnp.zeros_like(w_dt_s)
    w_dt_s[0:48, :] = w_dt_ref[...]
    dbl = (nt(act_s[...], w_dt_s[...]) + dbl_s[...]).astype(BF16)
    copies[2].wait()
    step_sum_s[...] = jnp.dot(dbl, w_xproj_ref[...], preferred_element_type=F32).reshape(T, PAD, C)
    for i in range(T):
        rows = slice(PAD * i, PAD * i + PAD)
        x_pre = x_pre_ref[rows, :]
        x_grad = x_sum_s[i] * step_ref[i] + grad_ref[i] * skip + step_sum_s[i]
        x_sig = jax.nn.sigmoid(x_pre)
        act_s[rows, :] = (x_grad * (x_sig * (1.0 + x_pre * (1.0 - x_sig)))).astype(BF16)
    copies[3].wait()
    token = (nt(act_s[...], w_in_ref[:, 0:C]) + nt(z_part_s[...], w_in_ref[:, C : 2 * C])).astype(
        BF16
    )
    for i in range(T):
        token_ref[i] = token[PAD * i : PAD * i + T, :]
    token_copy = pltpu.make_async_copy(token_ref, token_hbm, sems.at[5])
    token_copy.start()
    layer_copy.wait()
    token_copy.wait()


IN_VMEM = pl.BlockSpec(memory_space=pltpu.VMEM)
IN_HBM = pl.BlockSpec(memory_space=pltpu.HBM)


def call(kernel, out_shape, scratch, name, limit, *args, fetched=(), sent=()):
    many = isinstance(out_shape, tuple)
    return pl.pallas_call(
        kernel,
        out_shape=out_shape,
        in_specs=[IN_HBM if k in fetched else IN_VMEM for k in range(len(args))],
        out_specs=tuple(IN_HBM if k in sent else IN_VMEM for k in range(len(out_shape)))
        if many
        else IN_VMEM,
        scratch_shapes=scratch,
        name=name,
        compiler_params=pltpu.CompilerParams(vmem_limit_bytes=limit * 1024 * 1024),
    )(*args)


def f32(*shape):
    return jax.ShapeDtypeStruct(shape, F32)


def vmem(*shape):
    return pltpu.VMEM(shape, F32)


def prefix(axis, spans, sum_base, rows, got, sums, rates):
    def kernel(got_ref, sums_ref, rates_ref, out_ref):
        prefix_kernel(axis, spans, sum_base, got_ref, sums_ref, rates_ref, out_ref)

    out = f32(got.shape[0], rows, 128)
    return call(kernel, out, (), "prefix_" + axis, 4, got, sums, rates)


def swap(sent, axis, groups=None):
    return lax.all_to_all(sent, axis, 0, 0, tiled=True, axis_index_groups=groups)


def row_scan(own, got, sums, rates, reverse, gate=None):
    partner = [(place, place ^ 1) for place in range(16)]
    same_core = [[2 * chip + core for chip in range(8)] for core in range(2)]
    if sums is None:
        sums = (own, got)

    def combine(*refs):
        combine_kernel(reverse, *refs)

    def split(*refs):
        split_kernel(reverse, *refs)

    chip = call(
        combine, f32(8, own.shape[1], 128), (), "combine", 6, own, got, *sums[:2], rates
    )
    chips = swap(chip, "col", same_core)
    if gate is not None:
        rates = gate(chip)
    chip_sums = chips if len(sums) == 2 else sums[2]
    state = swap(
        prefix("col", ((0, reverse),), 72, 72, chips, chip_sums, rates), "col", same_core
    )
    half = f32(8, 72, 128)
    keep, send = call(split, (half, half), (), "split", 6, state, own, got, *sums[:2], rates)
    return keep, lax.ppermute(send, "col", partner), (*sums[:2], chip_sums)


def body(tokens, w_in, w_xproj, w_dt, dt_bias, a_log, d_skip, w_out, out_grad):
    edge, wide, dense = vmem(T, N, C), vmem(T, PAD, C), vmem(CELLS, C)
    flat, grid, spread = f32(CELLS, C), f32(T, PAD, C), f32(CELLS, N, 128)
    kept, sums, parts = vmem(T * T, N, C), vmem(PAD, C), vmem(C // 128, 8 * CELLS, 128)
    padded, cells = pltpu.VMEM((T, PAD, C), BF16), pltpu.VMEM((T, T, C), BF16)
    square, narrow = pltpu.VMEM((C, C), BF16), pltpu.VMEM((80, C), BF16)
    halves = vmem(8, 80, 128)
    low_rank, half_width = pltpu.VMEM((48, C), BF16), pltpu.VMEM((CELLS, C), BF16)
    w_xproj = w_xproj.T
    partner = [(place, place ^ 1) for place in range(16)]
    x_pre, dt_pre, step, u, x, b, c, rates, own, other = call(
        first_kernel,
        (flat, flat, grid, grid, flat, spread, spread, f32(N, C), f32(8, 80, 128), f32(8, 80, 128)),
        (
            dense, dense, wide, wide, dense, vmem(CELLS, N, 128), vmem(CELLS, N, 128),
            cells, square, narrow, low_rank, vmem(N, C),
            padded, edge, sums, vmem(N, C), halves, halves,
            pltpu.SemaphoreType.DMA((5,)), pltpu.SemaphoreType.DMA((10,)),
        ),
        "first", 54,
        tokens, w_in, w_xproj, w_dt, a_log, dt_bias,
        fetched=range(5), sent=range(10),
    )
    got = lax.ppermute(other, "col", partner)
    own, rates = call(
        stage_kernel, (f32(8, 80, 128), f32(N, C)), (), "stage", 4, own, rates
    )
    beside = []

    def gate(chip):
        out = call(
            gate_kernel, (flat, flat, grid, f32(T, N, C), f32(N, C)), (padded, padded), "gate", 54,
            chip, tokens, out_grad, w_in, w_out, step, c, rates,
            fetched=(0,),
        )
        beside.extend(out[:4])
        return out[4]

    keep, came, chip_sums = row_scan(own, got, None, rates, False, gate)
    z_pre, gated, grad, term = beside
    col_sent = call(
        forward_kernel, f32(16, 152, 128), (edge, edge, sums), "forward", 6,
        keep, came, rates, step, u, b, term,
    )
    col_all = swap(col_sent, "row")
    col_got = swap(
        prefix("row", ((0, False), (72, True)), 144, 144, col_all, col_all, rates), "row"
    )
    back_half = f32(8, 72, 128)
    back_own, back_other = call(
        backward_kernel, (back_half, back_half), (edge, edge), "backward", 6,
        col_got, rates, step, grad, c,
    )
    back_got = lax.ppermute(back_other, "col", partner)
    back_keep, back_came, chip_sums = row_scan(back_own, back_got, chip_sums, rates, True)
    out = jax.ShapeDtypeStruct((T, T, C), BF16)
    return call(
        last_kernel,
        (out, out),
        (
            pltpu.VMEM((C, 2 * C), BF16), narrow, low_rank, square, cells, cells,
            edge, edge, kept, kept, wide, wide, wide, vmem(CELLS, N, 128),
            vmem(CELLS, N, 128), parts, parts, narrow, half_width, half_width, vmem(CELLS, 80),
            pltpu.SemaphoreType.DMA((6,)),
        ),
        "last", 42,
        keep, came, col_got, back_keep, back_came, x_pre, z_pre, dt_pre, gated, step, u, x, grad, b, c, rates,
        d_skip, w_in, w_xproj, w_dt, w_out,
        fetched=range(17, 21), sent=range(2),
    )


def solution(mesh):
    return jax.shard_map(
        body,
        mesh=mesh,
        in_specs=(P("row", "col", None), P(), P(), P(), P(), P(), P(), P(), P("row", "col", None)),
        out_specs=(P("row", "col", None), P("row", "col", None)),
        check_vma=False,
    )
```
